768 devices in a mesh: dom: 32 (over z_lo, x, core), wf: 24 (over y, z_hi).
Axes of the slice: x: 4, y: 8, z: 12 (z_hi: 3, z_lo: 4; z = z_hi * 4 + z_lo), core: 2. Of those that a mesh axis runs over, the one named last changes fastest.
Arguments:
- wavefunctions: float32 [16384, 3072], P('dom', 'wf'), may hold values from -80 to 80
- cell_matrix: bfloat16 [64, 512, 512], P('dom'), may hold values from -1 to 4, as said below
- cell_nodes: int32 [64, 512], P('dom'), may hold values from 0 to 767, as said below
- home_counts: int32 [32, 3], P('dom'), may hold values from 0 to 4, as said below
- atom_start: int32 [32, 3, 4], P('dom'), may hold values from 0 to 256
- projectors: bfloat16 [32, 3, 4, 18, 256], P('dom'), may hold values from -0.375 to 0.375
- coupling: float32 [128, 18, 18], P('dom'), may hold values from -3 to 3
Outputs:
- filtered: float32 [16384, 3072], P('dom', 'wf')
- block_norm: float32 [], replicated
The draws below stay inside these ranges and needn't reach their ends.
Inputs may be any that keep to these rules, and one draw needn't show every extreme that they name: `cell_nodes`: each cell lists 512 distinct rows of its domain's extended numbering. home_counts[d, k] depends only on the home domain d - 1 + k and is the same on every domain that lists it; it is 0 for homes outside the grid and 1 to 4 otherwise. `cell_matrix`: each matrix is symmetric.
All inputs are finite; a program needn't handle non-finite values.
Results may differ from the reference program's by a relative error of at most 0.0056.
Values may be sent and summed in bfloat16 or wider, within the bound.
A program may use at most 32 MiB of HBM per device.

```python
import jax
import jax.numpy as jnp
from jax import lax

NPC = 512
CELL_DEV = 2
NPROJ = 18
SUP = 256
ATOM_HOME = 4
GHOST = 128
NODE_DEV = 512
EXT = 768
NODES = 16384
CELLS = 64
WF = 3072
ATOMS = 128
N_DOM = 32


def draw_wavefunctions(key, part):
    key_one, key_two, key_three = jax.random.split(key, 3)
    samples = jax.random.truncated_normal(key_one, -4.0, 4.0, (NODES, WF), jnp.float32)
    row_ramp = jnp.power(2.0, jnp.arange(NODES, dtype=jnp.float32) / NODES)
    row_scale = jnp.power(10.0, jax.random.uniform(key_two, (NODES,), jnp.float32, -0.5, 0.5)) * row_ramp
    column_ramp = jnp.power(2.0, jnp.arange(WF, dtype=jnp.float32) / WF)
    column_scale = jnp.power(10.0, jax.random.uniform(key_three, (WF,), jnp.float32, -0.5, 0.5)) * column_ramp
    return 0.5 * samples * row_scale[:, None] * column_scale[None, :]


def draw_cell_matrix(key, part):
    key_one, key_two = jax.random.split(key, 2)
    diagonal = jax.random.uniform(key_one, (CELLS, NPC), jnp.float32, 1.0, 3.0)
    off_diag = jax.random.truncated_normal(key_two, -4.0, 4.0, (CELLS, NPC, NPC), jnp.float32) * (0.8 / jnp.sqrt(NPC * 1.0))
    symmetric = 0.5 * (off_diag + jnp.swapaxes(off_diag, 1, 2))
    identity = jnp.eye(NPC, dtype=jnp.float32)
    return (symmetric * (1.0 - identity)[None] + diagonal[:, :, None] * identity[None]).astype(jnp.bfloat16)


def draw_cell_nodes(key, part):
    scores = jax.random.randint(key, (CELLS, NPC), 0, 1048576) * NPC + jnp.arange(NPC, dtype=jnp.int32)[None, :]
    orders = jnp.argsort(scores, axis=1).astype(jnp.int32)
    window_start = jnp.arange(CELLS, dtype=jnp.int32) % CELL_DEV * (NPC // 2)
    return (window_start[:, None] + orders).astype(jnp.int32)


def draw_home_counts(key, part):
    key_one, key_two = jax.random.split(jax.random.fold_in(key, 7), 2)
    counts = jax.random.randint(key_one, (N_DOM,), 1, ATOM_HOME + 1)
    busiest = jax.random.randint(key_two, (), 0, N_DOM)
    counts = jnp.where(jnp.arange(N_DOM, dtype=jnp.int32) == busiest, ATOM_HOME, counts).astype(jnp.int32)
    zero_count = jnp.zeros((1,), jnp.int32)
    padded = jnp.concatenate([zero_count, counts, zero_count], 0)
    return jnp.stack([padded[0:N_DOM], padded[1:N_DOM + 1], padded[2:N_DOM + 2]], 1).astype(jnp.int32)


def set_ends(result, key, smallest, largest):
    spot = [jax.random.randint(jax.random.fold_in(key, axis), (), 0, length) for axis, length in enumerate(result.shape)]
    widest = result.shape.index(max(result.shape))
    beside = spot[:widest] + [(spot[widest] + 1) % result.shape[widest]] + spot[widest + 1:]
    return result.at[tuple(spot)].set(smallest).at[tuple(beside)].set(largest)


def shard_levels(rng, extent, shards, least, top_value):
    loudness, own = 1.0, jax.random.fold_in(rng, 6)
    for position, blocks in shards:
        heights = jnp.exp(jax.random.uniform(jax.random.fold_in(own, position), (blocks,), jnp.float32, least / len(shards), top_value / len(shards)))
        loudness = loudness * jnp.repeat(heights, extent[position] // blocks).reshape([-1 if axis == position else 1 for axis in range(len(extent))])
    return loudness


def scatter_about(rng, dims, scale, bound, cuts=(), kind=jnp.bfloat16):
    gain = shard_levels(rng, dims, cuts, -0.22, 0.18) if cuts else 1.0
    drawn = jax.random.normal(rng, dims, jnp.float32) * scale * gain
    return jnp.minimum(jnp.maximum(drawn, -bound), bound).astype(kind)


def setup_inputs(seed: int = 0) -> dict:
    keys = jax.random.split(jax.random.key(seed), 8)
    return {
        "wavefunctions": draw_wavefunctions(jax.random.fold_in(keys[7], 71), 0),
        "cell_matrix": draw_cell_matrix(jax.random.fold_in(keys[7], 71), 0),
        "cell_nodes": draw_cell_nodes(jax.random.fold_in(keys[7], 71), 0),
        "home_counts": draw_home_counts(jax.random.fold_in(keys[7], 71), 0),
        "atom_start": set_ends(jax.random.randint(keys[4], (N_DOM, 3, ATOM_HOME), 0, NODE_DEV - SUP + 1), jax.random.fold_in(keys[4], 1), 0, NODE_DEV - SUP).astype(jnp.int32),
        "projectors": scatter_about(keys[5], (N_DOM, 3, ATOM_HOME, NPROJ, SUP), SUP ** -0.5, 0.375, ((0, 32),)),
        "coupling": scatter_about(keys[6], (ATOMS, NPROJ, NPROJ), 0.5, 3.0, ((0, 32),), jnp.float32),
    }


lower_edge = -1.0
cut_edge = 2.0
upper_edge = 9.0

def apply_hamiltonian(vector, cell_matrix, cell_nodes, home_counts, atom_start, projectors, coupling):
    rounded = vector.astype(jnp.bfloat16)
    padded = jnp.pad(rounded, ((GHOST, GHOST), (0, 0)))
    domains = jnp.arange(N_DOM, dtype=jnp.int32)
    matrices = cell_matrix.reshape(N_DOM, CELL_DEV, NPC, NPC)
    node_lists = cell_nodes.reshape(N_DOM, CELL_DEV, NPC)

    def one_domain(inputs):
        domain_index, domain_mats, domain_lists = inputs
        extended = lax.dynamic_slice_in_dim(padded, (domain_index * NODE_DEV).astype(jnp.int32), EXT, 0)
        gathered = extended[domain_lists]
        products = jnp.einsum('cij,cjw->ciw', domain_mats.astype(jnp.float32), gathered.astype(jnp.float32))
        return jnp.zeros((EXT, WF), jnp.float32).at[domain_lists.reshape(-1)].add(products.reshape(-1, WF))
    pieces = lax.map(one_domain, (domains, matrices, node_lists))
    owned = pieces[:, GHOST:GHOST + NODE_DEV]
    owned = owned.at[1:, :GHOST].add(pieces[:-1, EXT - GHOST:])
    owned = owned.at[:-1, NODE_DEV - GHOST:].add(pieces[1:, :GHOST])
    cell_part = owned.reshape(NODES, WF)
    blocks = rounded.reshape(N_DOM, NODE_DEV, WF)
    live = (jnp.arange(ATOM_HOME, dtype=jnp.int32)[None, None, :] < home_counts[:, :, None]).astype(jnp.float32)
    offsets = jnp.arange(SUP, dtype=jnp.int32)

    def project(inputs):
        domain_block, starts, projector_block, slot_mask = inputs
        slot_rows = starts.reshape(-1)[:, None] + offsets[None, :]
        windows = domain_block[slot_rows]
        flat = projector_block.reshape(3 * ATOM_HOME, NPROJ, SUP)
        coefficients = jnp.einsum('spn,snw->spw', flat.astype(jnp.float32), windows.astype(jnp.float32))
        return coefficients * slot_mask.reshape(-1)[:, None, None]
    partial_value = lax.map(project, (blocks, atom_start, projectors, live))
    partial_value = partial_value.reshape(N_DOM, 3, ATOM_HOME, NPROJ, WF)
    zero_block = jnp.zeros((1, ATOM_HOME, NPROJ, WF), jnp.float32)
    home_sum = partial_value[:, 1] + jnp.concatenate([partial_value[1:, 0], zero_block], 0) + jnp.concatenate([zero_block, partial_value[:-1, 2]], 0)
    atom_values = jnp.einsum('hapq,haqw->hapw', coupling.reshape(N_DOM, ATOM_HOME, NPROJ, NPROJ), home_sum, precision=lax.Precision.HIGHEST).astype(jnp.bfloat16)
    zero_values = jnp.zeros((1, ATOM_HOME, NPROJ, WF), jnp.bfloat16)
    padded_values = jnp.concatenate([zero_values, atom_values, zero_values], 0)
    slot_values = jnp.stack([padded_values[0:N_DOM], padded_values[1:N_DOM + 1], padded_values[2:N_DOM + 2]], 1)

    def spread(inputs):
        starts, projector_block, values_block, slot_mask = inputs
        slot_rows = starts.reshape(-1)[:, None] + offsets[None, :]
        flat = projector_block.reshape(3 * ATOM_HOME, NPROJ, SUP)
        flat_values = values_block.reshape(3 * ATOM_HOME, NPROJ, WF)
        contributions = jnp.einsum('spn,spw->snw', flat.astype(jnp.float32), flat_values.astype(jnp.float32))
        contributions = contributions * slot_mask.reshape(-1)[:, None, None]
        return jnp.zeros((NODE_DEV, WF), jnp.float32).at[slot_rows.reshape(-1)].add(contributions.reshape(-1, WF))
    projected_part = lax.map(spread, (atom_start, projectors, slot_values, live)).reshape(NODES, WF)
    return cell_part + projected_part

def reference(wavefunctions, cell_matrix, cell_nodes, home_counts, atom_start, projectors, coupling):
    half_width = (upper_edge - cut_edge) / 2.0
    centre = (upper_edge + cut_edge) / 2.0
    sigma_one = half_width / (lower_edge - centre)
    gamma_ratio = 2.0 / sigma_one

    def shifted(vector):
        return apply_hamiltonian(vector, cell_matrix, cell_nodes, home_counts, atom_start, projectors, coupling) - centre * vector
    order_one = shifted(wavefunctions) * (sigma_one / half_width)
    sigma_two = 1.0 / (gamma_ratio - sigma_one)
    order_two = shifted(order_one) * (2.0 * sigma_two / half_width) - sigma_one * sigma_two * wavefunctions
    sigma_three = 1.0 / (gamma_ratio - sigma_two)
    filtered = shifted(order_two) * (2.0 * sigma_three / half_width) - sigma_two * sigma_three * order_one
    block_norm = jnp.sqrt(jnp.sum(filtered * filtered))
    return (filtered, block_norm)
```

```python
import functools

import jax
import jax.numpy as jnp
from jax import lax
from jax.experimental import pallas as pl
from jax.experimental.pallas import tpu as pltpu
from jax.sharding import PartitionSpec as P

F32, BF16 = jnp.float32, jnp.bfloat16
MESH = pl.DeviceIdType.MESH

lower_edge = -1.0
cut_edge = 2.0
upper_edge = 9.0

CELLS = 2
NPC = 512
OWN = 512
GHOST = 128
EXT = OWN + 2 * GHOST
COLS = 128
NPROJ, SUP, ATOM_HOME = 18, 256, 4
SLOT = 24
HOME = 80
PROWS = 3 * HOME
GROWS = 2 * GHOST + PROWS
BLK = GHOST + 2 * HOME
LO = GHOST + PROWS
ROW, PLANE, ZLO = 8, 3, 4


def dot(a, b):
    return jnp.dot(a, b, preferred_element_type=F32)


def dot_nt(a, b):
    return lax.dot_general(a, b, (((1,), (1,)), ((), ())), preferred_element_type=F32)


def dot_tn(a, b):
    return lax.dot_general(a, b, (((0,), (0,)), ((), ())), preferred_element_type=F32)


def kernel(
    ny,
    wave_ref, matrix_ref, nodes_ref, counts_ref, starts_ref, proj_ref, coupling_ref,
    out_ref, norm_ref,
    fv, vb, gb, xb, rblk, rc2, c32, acc,
    cm, scat, tcat, gmat, ahi, alo, fmat, corner, csend, crecv,
    pin, pst, pall, cin, cst, csn, crc, call,
    part, ysum, zsum,
    in_sem, out_sem, send_sem, recv_sem, ssend_sem, srecv_sem,
    nsend, nrecv,
):
    d, w = lax.axis_index("dom"), lax.axis_index("wf")
    n_dom = 32
    below1, below2, above1, above2 = d >= 1, d >= 2, d < n_dom - 1, d < n_dom - 2

    loads = [
        pltpu.make_async_copy(proj_ref, pin, in_sem.at[0]),
        pltpu.make_async_copy(coupling_ref, cin, in_sem.at[1]),
        pltpu.make_async_copy(matrix_ref, cm, in_sem.at[2]),
        pltpu.make_async_copy(wave_ref, fv.at[0], in_sem.at[3]),
    ]
    for load in loads:
        load.start()

    zlo, row = lax.div(d, ROW), lax.rem(d, ROW)
    y, zhi = lax.div(w, PLANE), lax.rem(w, PLANE)
    z = zhi * ZLO + zlo
    nz = ZLO * PLANE

    def row_peer(k):
        i = lax.rem(row + k, ROW)
        return i, (zlo * ROW + i, w)

    def y_peer(k):
        i = lax.rem(y + k, ny)
        return i, (d, i * PLANE + zhi)

    def z_peer(k):
        i = lax.rem(z + k, nz)
        return i, (lax.rem(i, ZLO) * ROW + row, y * PLANE + lax.div(i, ZLO))

    stages = ((ROW, row_peer, row), (ny, y_peer, y), (nz, z_peer, z))

    barrier = pltpu.get_barrier_semaphore()
    for cond, other in ((below1, d - 1), (above1, d + 1), (below2, d - 2), (above2, d + 2)):
        @pl.when(cond)
        def _():
            pl.semaphore_signal(barrier, inc=1, device_id=(other, w), device_id_type=MESH)
    for size, peer, _ in stages:
        for k in range(1, size):
            pl.semaphore_signal(barrier, inc=1, device_id=peer(k)[1], device_id_type=MESH)

    def zero(ref):
        ref[...] = jnp.zeros(ref.shape, ref.dtype)

    for a in range(3):
        zero(xb.at[a, pl.ds(OWN, EXT - OWN)])
    for cond, refs in (
        (below1, lambda: [rblk.at[a, 0] for a in range(3)] + [xb.at[a, pl.ds(GHOST, GHOST)] for a in range(3)] + [crecv.at[0], crc.at[0]]),
        (above1, lambda: [rblk.at[a, 1] for a in range(3)] + [xb.at[a, pl.ds(2 * GHOST, GHOST)] for a in range(3)] + [crecv.at[1], crc.at[1]]),
        (below2, lambda: [rc2.at[a, 0] for a in range(3)] + [xb.at[a, pl.ds(0, GHOST)] for a in range(3)]),
        (above2, lambda: [rc2.at[a, 1] for a in range(3)] + [xb.at[a, pl.ds(3 * GHOST, GHOST)] for a in range(3)]),
    ):
        @pl.when(jnp.logical_not(cond))
        def _():
            for ref in refs():
                zero(ref)
    zero(pst)
    zero(cst)
    zero(fmat.at[pl.ds(GHOST, OWN - GHOST), pl.ds(0, GHOST)])
    zero(fmat.at[pl.ds(0, OWN - GHOST), pl.ds(3 * GHOST, GHOST)])

    for c in range(CELLS):
        nodes = nodes_ref[pl.ds(c, 1), :]
        rows = lax.broadcasted_iota(jnp.int32, (EXT, NPC), 0)
        scat[:, c * NPC:(c + 1) * NPC] = jnp.where(rows == nodes, 1.0, 0.0).astype(BF16)

    loads[0].wait()
    for k in range(3):
        for j in range(ATOM_HOME):
            i = (k * ATOM_HOME + j) * SLOT
            pst[pl.ds(i, NPROJ), pl.ds(0, SUP)] = pin[0, k, j].astype(F32)
            live = jnp.where(j < counts_ref[0, k], 1.0, 0.0).astype(F32)
            placed = pltpu.roll(pst[pl.ds(i, SLOT), :], starts_ref[0, k, j], axis=1)
            pst[pl.ds(i, SLOT), :] = placed * live
    pall[...] = pst[...].astype(BF16)
    col = lax.broadcasted_iota(jnp.int32, (1, 3 * ATOM_HOME * SLOT), 1)
    slot, p = lax.div(col, SLOT), lax.rem(col, SLOT)
    target = lax.div(slot, ATOM_HOME) * HOME + lax.rem(slot, ATOM_HOME) * NPROJ + p
    target = jnp.where(p < NPROJ, target, -1)
    pick = jnp.where(
        lax.broadcasted_iota(jnp.int32, (PROWS, 3 * ATOM_HOME * SLOT), 0) == target, 1.0, 0.0
    ).astype(BF16)
    gmat[pl.ds(GHOST, PROWS), :] = dot(pick, pall[...]).astype(BF16)

    loads[1].wait()
    for j in range(ATOM_HOME):
        cst[pl.ds(j * SLOT, NPROJ), pl.ds(0, NPROJ)] = cin[j]
        rows = cst[pl.ds(j * SLOT, SLOT), :]
        csn[pl.ds(j * SLOT, SLOT), :] = rows if j == 0 else pltpu.roll(rows, j * NPROJ, axis=1)

    loads[2].wait()

    def assemble(start, rows):
        for c in range(CELLS):
            tcat[pl.ds(start, rows), c * NPC:(c + 1) * NPC] = dot(
                scat[pl.ds(start, rows), c * NPC:(c + 1) * NPC], cm[c]
            ).astype(BF16)
        return dot_nt(tcat[pl.ds(start, rows), :], scat[...])

    for side, start, grow in ((0, 0, 0), (1, GHOST + OWN, LO)):
        rim = assemble(start, GHOST)
        gmat[pl.ds(grow, GHOST), :] = rim[:, GHOST:GHOST + OWN].astype(BF16)
        csend[side, :, 0:GHOST] = rim[:, 0:GHOST].astype(BF16)
        csend[side, :, GHOST:2 * GHOST] = rim[:, GHOST + OWN:].astype(BF16)

    loads[3].wait()
    vb[0] = fv[0].astype(BF16)

    def remote(src, dst, sems, other):
        return pltpu.make_async_remote_copy(
            src_ref=src, dst_ref=dst, send_sem=sems[0], recv_sem=sems[1],
            device_id=(other, w), device_id_type=MESH,
        )

    def app_copies(a):
        def sems(i):
            return send_sem.at[a, i], recv_sem.at[a, i]

        low, high = vb.at[a, pl.ds(0, GHOST)], vb.at[a, pl.ds(OWN - GHOST, GHOST)]
        edges = [
            (above1, below1, high, xb.at[a, pl.ds(GHOST, GHOST)], sems(0), d + 1),
            (below1, above1, low, xb.at[a, pl.ds(2 * GHOST, GHOST)], sems(4), d - 1),
            (above2, below2, high, xb.at[a, pl.ds(0, GHOST)], sems(2), d + 2),
            (below2, above2, low, xb.at[a, pl.ds(3 * GHOST, GHOST)], sems(6), d - 2),
        ]
        blocks = [
            (above1, below1, gb.at[a, pl.ds(GHOST + HOME, BLK)], rblk.at[a, 0], sems(1), d + 1),
            (below1, above1, gb.at[a, pl.ds(0, BLK)], rblk.at[a, 1], sems(5), d - 1),
            (above2, below2, gb.at[a, pl.ds(GHOST + 2 * HOME, HOME)], rc2.at[a, 0], sems(3), d + 2),
            (below2, above2, gb.at[a, pl.ds(GHOST, HOME)], rc2.at[a, 1], sems(7), d - 2),
        ]
        return edges, blocks

    def setup_copies():
        def sems(i):
            return ssend_sem.at[i], srecv_sem.at[i]

        return [
            (above1, below1, csend.at[1], crecv.at[0], sems(0), d + 1),
            (below1, above1, csend.at[0], crecv.at[1], sems(1), d - 1),
            (above1, below1, csn, crc.at[0], sems(2), d + 1),
            (below1, above1, csn, crc.at[1], sems(3), d - 1),
        ]

    def start(copies):
        for cond, _, src, dst, sems, other in copies:
            @pl.when(cond)
            def _():
                remote(src, dst, sems, other).start()

    def wait_recv(copies):
        for _, cond, src, dst, sems, other in copies:
            @pl.when(cond)
            def _():
                remote(src, dst, sems, other).wait_recv()

    def wait_send(copies):
        for cond, _, src, dst, sems, other in copies:
            @pl.when(cond)
            def _():
                remote(src, dst, sems, other).wait_send()

    def project(a):
        g = dot(gmat[...], vb[a])
        gb[a] = g.astype(BF16)
        c32[...] = g[GHOST:LO]

    project(0)

    pl.semaphore_wait(
        barrier,
        (ROW + ny + nz - 3) + below1.astype(jnp.int32) + below2.astype(jnp.int32)
        + above1.astype(jnp.int32) + above2.astype(jnp.int32),
    )
    for group in app_copies(0):
        start(group)
    start(setup_copies())

    def split(block, rows, cols):
        high = block.astype(BF16)
        ahi[rows, cols] = high
        alo[rows, cols] = (block - high.astype(F32)).astype(BF16)

    for q in range(4):
        rows = pl.ds(q * GHOST, GHOST)
        body = assemble((q + 1) * GHOST, GHOST)
        split(body[:, GHOST:GHOST + OWN], rows, pl.ds(0, OWN))
        if q == 0:
            corner[0] = body[:, GHOST:2 * GHOST]
        if q == 3:
            corner[1] = body[:, OWN:OWN + GHOST]
        fmat[rows, GHOST:2 * GHOST] = body[:, 0:GHOST].astype(BF16)
        fmat[rows, 2 * GHOST:3 * GHOST] = body[:, GHOST + OWN:].astype(BF16)

    wait_recv(setup_copies())
    fmat[0:GHOST, 0:GHOST] = crecv[0, :, 0:GHOST]
    fmat[OWN - GHOST:, 3 * GHOST:4 * GHOST] = crecv[1, :, GHOST:]
    low, high = pl.ds(0, GHOST), pl.ds(OWN - GHOST, GHOST)
    split(corner[0] + crecv[0, :, GHOST:].astype(F32), low, low)
    split(corner[1] + crecv[1, :, 0:GHOST].astype(F32), high, high)
    empty = jnp.zeros((ATOM_HOME * SLOT, 128), F32)
    for k, block in ((0, crc[0]), (1, csn[...]), (2, crc[1])):
        wide = jnp.concatenate([block, empty], axis=1)
        call[pl.ds(k * ATOM_HOME * SLOT, ATOM_HOME * SLOT), :] = wide if k == 0 else pltpu.roll(wide, k * HOME, axis=1)
    couple = call[...]
    couple_hi = couple.astype(BF16)
    couple_lo = (couple - couple_hi.astype(F32)).astype(BF16)
    fmat[:, OWN:] = (dot_tn(pall[...], couple_hi) + dot_tn(pall[...], couple_lo)).astype(BF16)

    half_width = (upper_edge - cut_edge) / 2.0
    centre = (upper_edge + cut_edge) / 2.0
    sigma_one = half_width / (lower_edge - centre)
    gamma_ratio = 2.0 / sigma_one
    sigma_two = 1.0 / (gamma_ratio - sigma_one)
    sigma_three = 1.0 / (gamma_ratio - sigma_two)
    scales = (sigma_one / half_width, 2.0 * sigma_two / half_width, 2.0 * sigma_three / half_width)
    backs = (0.0, sigma_one * sigma_two, sigma_two * sigma_three)

    for a in range(3):
        edges, blocks = app_copies(a)
        if a > 0:
            start(edges)
            project(a)
            start(blocks)
        acc[...] = dot(ahi[...], vb[a]) + dot(alo[...], vb[a]) - centre * fv[a]
        wait_recv(edges)
        wait_recv(blocks)
        below, above = rblk[a, 0].astype(F32), rblk[a, 1].astype(F32)
        own = c32[...]
        xb[a, OWN:OWN + HOME, :] = (own[0:HOME] + below[0:HOME] + rc2[a, 0].astype(F32)).astype(BF16)
        xb[a, OWN + HOME:OWN + 2 * HOME, :] = (
            own[HOME:2 * HOME] + below[HOME:2 * HOME] + above[GHOST:GHOST + HOME]
        ).astype(BF16)
        xb[a, OWN + 2 * HOME:OWN + 3 * HOME, :] = (
            own[2 * HOME:] + above[GHOST + HOME:] + rc2[a, 1].astype(F32)
        ).astype(BF16)
        acc[0:GHOST, :] += below[2 * HOME:]
        acc[OWN - GHOST:, :] += above[0:GHOST]
        new = (acc[...] + dot(fmat[...], xb[a])) * scales[a]
        if a > 0:
            new = new - backs[a] * fv[a - 1]
        fv[a + 1] = new
        if a < 2:
            vb[a + 1] = new.astype(BF16)

    result = fv.at[3]
    store = pltpu.make_async_copy(result, out_ref, out_sem)
    store.start()

    mine = jnp.sum(fv[3] * fv[3], axis=0, keepdims=True)
    base = 0
    for (size, peer, me), sums in zip(stages, (part, ysum, zsum)):
        sums[me] = mine
        copies = []
        for k in range(1, size):
            i, where = peer(k)
            copies.append(pltpu.make_async_remote_copy(
                src_ref=sums.at[me], dst_ref=sums.at[me],
                send_sem=nsend.at[base + k], recv_sem=nrecv.at[base + me],
                device_id=where, device_id_type=MESH,
            ))
        for copy in copies:
            copy.start()
        for k in range(1, size):
            i, where = peer(k)
            pltpu.make_async_remote_copy(
                src_ref=sums.at[i], dst_ref=sums.at[i],
                send_sem=nsend.at[base + k], recv_sem=nrecv.at[base + i],
                device_id=where, device_id_type=MESH,
            ).wait_recv()
        mine = sums[0]
        for i in range(1, size):
            mine = mine + sums[i]
        for copy in copies:
            copy.wait_send()
        base += size
    norm_ref[0, 0] = jnp.sqrt(jnp.sum(mine, axis=1, keepdims=True))[0, 0]

    for a in range(3):
        for group in app_copies(a):
            wait_send(group)
    wait_send(setup_copies())
    store.wait()


def solution(mesh):
    ny = mesh.shape["wf"] // PLANE
    members = ROW + ny + ZLO * PLANE

    def local(wavefunctions, cell_matrix, cell_nodes, home_counts, atom_start, projectors, coupling):
        hbm = pl.BlockSpec(memory_space=pl.ANY)
        vmem = pl.BlockSpec(memory_space=pltpu.VMEM)
        smem = pl.BlockSpec(memory_space=pltpu.SMEM)
        filtered, norm = pl.pallas_call(
            functools.partial(kernel, ny),
            out_shape=(
                jax.ShapeDtypeStruct((OWN, COLS), F32),
                jax.ShapeDtypeStruct((1, 1), F32),
            ),
            in_specs=[hbm, hbm, vmem, smem, smem, hbm, hbm],
            out_specs=(hbm, smem),
            scratch_shapes=[
                pltpu.VMEM((4, OWN, COLS), F32),
                pltpu.VMEM((3, OWN, COLS), BF16),
                pltpu.VMEM((3, GROWS, COLS), BF16),
                pltpu.VMEM((3, EXT, COLS), BF16),
                pltpu.VMEM((3, 2, BLK, COLS), BF16),
                pltpu.VMEM((3, 2, HOME, COLS), BF16),
                pltpu.VMEM((PROWS, COLS), F32),
                pltpu.VMEM((OWN, COLS), F32),
                pltpu.VMEM((CELLS, NPC, NPC), BF16),
                pltpu.VMEM((EXT, CELLS * NPC), BF16),
                pltpu.VMEM((EXT, CELLS * NPC), BF16),
                pltpu.VMEM((GROWS, OWN), BF16),
                pltpu.VMEM((OWN, OWN), BF16),
                pltpu.VMEM((OWN, OWN), BF16),
                pltpu.VMEM((OWN, EXT), BF16),
                pltpu.VMEM((2, GHOST, GHOST), F32),
                pltpu.VMEM((2, GHOST, 2 * GHOST), BF16),
                pltpu.VMEM((2, GHOST, 2 * GHOST), BF16),
                pltpu.VMEM((1, 3, ATOM_HOME, NPROJ, SUP), BF16),
                pltpu.VMEM((3 * ATOM_HOME * SLOT, OWN), F32),
                pltpu.VMEM((3 * ATOM_HOME * SLOT, OWN), BF16),
                pltpu.VMEM((ATOM_HOME, NPROJ, NPROJ), F32),
                pltpu.VMEM((ATOM_HOME * SLOT, 128), F32),
                pltpu.VMEM((ATOM_HOME * SLOT, 128), F32),
                pltpu.VMEM((2, ATOM_HOME * SLOT, 128), F32),
                pltpu.VMEM((3 * ATOM_HOME * SLOT, 256), F32),
                pltpu.VMEM((ROW, 1, COLS), F32),
                pltpu.VMEM((ny, 1, COLS), F32),
                pltpu.VMEM((ZLO * PLANE, 1, COLS), F32),
                pltpu.SemaphoreType.DMA((4,)),
                pltpu.SemaphoreType.DMA,
                pltpu.SemaphoreType.DMA((3, 8)),
                pltpu.SemaphoreType.DMA((3, 8)),
                pltpu.SemaphoreType.DMA((4,)),
                pltpu.SemaphoreType.DMA((4,)),
                pltpu.SemaphoreType.DMA((members,)),
                pltpu.SemaphoreType.DMA((members,)),
            ],
            compiler_params=pltpu.CompilerParams(collective_id=0, has_side_effects=True),
            name="chebyshev",
        )(wavefunctions, cell_matrix, cell_nodes, home_counts, atom_start, projectors, coupling)
        return filtered, norm.reshape(())

    return jax.shard_map(
        local,
        mesh=mesh,
        in_specs=(
            P("dom", "wf"),
            P("dom", None, None),
            P("dom", None),
            P("dom", None),
            P("dom", None, None),
            P("dom", None, None, None, None),
            P("dom", None, None),
        ),
        out_specs=(P("dom", "wf"), P()),
        check_vma=False,
    )
```

```python
import functools

import jax
import jax.numpy as jnp
from jax import lax
from jax.experimental import pallas as pl
from jax.experimental.pallas import tpu as pltpu
from jax.sharding import PartitionSpec as P

F32, BF16 = jnp.float32, jnp.bfloat16
MESH = pl.DeviceIdType.MESH

lower_edge = -1.0
cut_edge = 2.0
upper_edge = 9.0

CELLS = 2
NPC = 512
OWN = 512
GHOST = 128
EXT = OWN + 2 * GHOST
COLS = 128
NPROJ, SUP, ATOM_HOME = 18, 256, 4
SLOT = 24
HOME = 80
PROWS = 3 * HOME
GROWS = 2 * GHOST + PROWS
BLK = GHOST + 2 * HOME
LO = GHOST + PROWS
ROW, PLANE, ZLO = 8, 3, 4


def dot(a, b):
    return jnp.dot(a, b, preferred_element_type=F32)


def dot_nt(a, b):
    return lax.dot_general(a, b, (((1,), (1,)), ((), ())), preferred_element_type=F32)


def dot_tn(a, b):
    return lax.dot_general(a, b, (((0,), (0,)), ((), ())), preferred_element_type=F32)


def kernel(
    ny,
    wave_ref, matrix_ref, nodes_ref, counts_ref, starts_ref, proj_ref, coupling_ref,
    out_ref, norm_ref,
    fv, vb, gb, xb, rblk, rc2, c32, acc,
    cm, scat, tcat, gmat, amat, dtab, fmat, corner, csend, crecv,
    pin, pst, pall, cin, cst, csn, crc, call,
    part, ysum, zsum,
    in_sem, out_sem, send_sem, recv_sem, ssend_sem, srecv_sem,
    nsend, nrecv,
):
    d, w = lax.axis_index("dom"), lax.axis_index("wf")
    n_dom = 32
    below1, below2, above1, above2 = d >= 1, d >= 2, d < n_dom - 1, d < n_dom - 2

    loads = [
        pltpu.make_async_copy(proj_ref, pin, in_sem.at[0]),
        pltpu.make_async_copy(coupling_ref, cin, in_sem.at[1]),
        pltpu.make_async_copy(matrix_ref, cm, in_sem.at[2]),
        pltpu.make_async_copy(wave_ref, fv.at[0], in_sem.at[3]),
    ]
    for i in (2, 0, 3, 1):
        loads[i].start()

    zlo, row = lax.div(d, ROW), lax.rem(d, ROW)
    y, zhi = lax.div(w, PLANE), lax.rem(w, PLANE)
    z = zhi * ZLO + zlo
    nz = ZLO * PLANE

    def around(i, size):
        return i - size * (i >= size).astype(jnp.int32)

    def row_peer(k):
        i = around(row + k, ROW)
        return i, (zlo * ROW + i, w)

    def y_peer(k):
        i = around(y + k, ny)
        return i, (d, i * PLANE + zhi)

    def z_peer(k):
        i = around(z + k, nz)
        hi = (i >= ZLO).astype(jnp.int32) + (i >= 2 * ZLO).astype(jnp.int32)
        return i, ((i - ZLO * hi) * ROW + row, y * PLANE + hi)

    def far_first(size):
        return sorted(range(1, size), key=lambda k: -min(k, size - k))

    stages = ((ROW, row_peer, row), (ny, y_peer, y), (nz, z_peer, z))

    barrier = pltpu.get_barrier_semaphore()
    for cond, other in ((below1, d - 1), (above1, d + 1), (below2, d - 2), (above2, d + 2)):
        @pl.when(cond)
        def _():
            pl.semaphore_signal(barrier, inc=1, device_id=(other, w), device_id_type=MESH)
    for size, peer, _ in stages:
        for k in far_first(size):
            pl.semaphore_signal(barrier, inc=1, device_id=peer(k)[1], device_id_type=MESH)

    def zero(ref):
        ref[...] = jnp.zeros(ref.shape, ref.dtype)

    for a in range(3):
        zero(xb.at[a, pl.ds(OWN, EXT - OWN)])
    for cond, refs in (
        (below1, lambda: [rblk.at[a, 0] for a in range(3)] + [xb.at[a, pl.ds(GHOST, GHOST)] for a in range(3)] + [crecv.at[0], crc.at[0]]),
        (above1, lambda: [rblk.at[a, 1] for a in range(3)] + [xb.at[a, pl.ds(2 * GHOST, GHOST)] for a in range(3)] + [crecv.at[1], crc.at[1]]),
        (below2, lambda: [rc2.at[a, 0] for a in range(3)] + [xb.at[a, pl.ds(0, GHOST)] for a in range(3)]),
        (above2, lambda: [rc2.at[a, 1] for a in range(3)] + [xb.at[a, pl.ds(3 * GHOST, GHOST)] for a in range(3)]),
    ):
        @pl.when(jnp.logical_not(cond))
        def _():
            for ref in refs():
                zero(ref)
    zero(pst)
    zero(cst)
    zero(fmat.at[pl.ds(GHOST, OWN - GHOST), pl.ds(0, GHOST)])
    zero(fmat.at[pl.ds(0, OWN - GHOST), pl.ds(3 * GHOST, GHOST)])

    for c in range(CELLS):
        nodes = nodes_ref[pl.ds(c, 1), :]
        nodes = jnp.where(nodes < GHOST, nodes, jnp.where(nodes >= GHOST + OWN, nodes - OWN, nodes + GHOST))
        rows = lax.broadcasted_iota(jnp.int32, (EXT, NPC), 0)
        scat[:, c * NPC:(c + 1) * NPC] = jnp.where(rows == nodes, 1.0, 0.0).astype(BF16)

    loads[0].wait()
    for k in range(3):
        for j in range(ATOM_HOME):
            i = (k * ATOM_HOME + j) * SLOT
            pst[pl.ds(i, NPROJ), pl.ds(0, SUP)] = pin[0, k, :, j, :].astype(F32)
            live = jnp.where(j < counts_ref[0, k], 1.0, 0.0).astype(F32)
            placed = pltpu.roll(pst[pl.ds(i, SLOT), :], starts_ref[k, 0, j], axis=1)
            pst[pl.ds(i, SLOT), :] = placed * live
    pall[...] = pst[...].astype(BF16)
    col = lax.broadcasted_iota(jnp.int32, (1, 3 * ATOM_HOME * SLOT), 1)
    slot, p = lax.div(col, SLOT), lax.rem(col, SLOT)
    target = lax.div(slot, ATOM_HOME) * HOME + lax.rem(slot, ATOM_HOME) * NPROJ + p
    target = jnp.where(p < NPROJ, target, -1)
    pick = jnp.where(
        lax.broadcasted_iota(jnp.int32, (PROWS, 3 * ATOM_HOME * SLOT), 0) == target, 1.0, 0.0
    ).astype(BF16)
    gmat[pl.ds(GHOST, PROWS), :] = dot(pick, pall[...]).astype(BF16)

    loads[1].wait()
    for j in range(ATOM_HOME):
        cst[pl.ds(j * SLOT, NPROJ), pl.ds(0, NPROJ)] = cin[:, j, :]
        rows = cst[pl.ds(j * SLOT, SLOT), :]
        csn[pl.ds(j * SLOT, SLOT), :] = rows if j == 0 else pltpu.roll(rows, j * NPROJ, axis=1)

    loads[2].wait()

    rims = 2 * GHOST
    eye = lax.broadcasted_iota(jnp.int32, (GHOST, GHOST), 0) == lax.broadcasted_iota(jnp.int32, (GHOST, GHOST), 1)

    def place(rows):
        for c in range(CELLS):
            cell = pl.ds(c * NPC, NPC)
            tcat[rows, cell] = dot(scat[rows, cell], cm[c]).astype(BF16)

    place(pl.ds(0, rims))
    rim = dot_nt(tcat[0:rims, :], scat[...])
    gmat[pl.ds(0, GHOST), :] = rim[0:GHOST, rims:].astype(BF16)
    gmat[pl.ds(LO, GHOST), :] = rim[GHOST:, rims:].astype(BF16)
    for side in range(2):
        ends = rim[side * GHOST:(side + 1) * GHOST, 0:rims]
        rounded = ends.astype(BF16)
        csend[side, 0:GHOST, :] = rounded
        left = (ends - rounded.astype(F32))[:, side * GHOST:(side + 1) * GHOST]
        left = jnp.sum(jnp.where(eye, left, 0.0), axis=0, keepdims=True)
        csend[side, GHOST:, 0:GHOST] = jnp.broadcast_to(left, (16, GHOST)).astype(BF16)

    loads[3].wait()
    vb[0] = fv[0].astype(BF16)

    def remote(src, dst, sems, other):
        return pltpu.make_async_remote_copy(
            src_ref=src, dst_ref=dst, send_sem=sems[0], recv_sem=sems[1],
            device_id=(other, w), device_id_type=MESH,
        )

    def app_copies(a):
        def sems(i):
            return send_sem.at[a, i], recv_sem.at[a, i]

        low, high = vb.at[a, pl.ds(0, GHOST)], vb.at[a, pl.ds(OWN - GHOST, GHOST)]
        edges = [
            (above1, below1, high, xb.at[a, pl.ds(GHOST, GHOST)], sems(0), d + 1),
            (below1, above1, low, xb.at[a, pl.ds(2 * GHOST, GHOST)], sems(4), d - 1),
            (above2, below2, high, xb.at[a, pl.ds(0, GHOST)], sems(2), d + 2),
            (below2, above2, low, xb.at[a, pl.ds(3 * GHOST, GHOST)], sems(6), d - 2),
        ]
        blocks = [
            (above1, below1, gb.at[a, pl.ds(GHOST + HOME, BLK)], rblk.at[a, 0], sems(1), d + 1),
            (below1, above1, gb.at[a, pl.ds(0, BLK)], rblk.at[a, 1], sems(5), d - 1),
            (above2, below2, gb.at[a, pl.ds(GHOST + 2 * HOME, HOME)], rc2.at[a, 0], sems(3), d + 2),
            (below2, above2, gb.at[a, pl.ds(GHOST, HOME)], rc2.at[a, 1], sems(7), d - 2),
        ]
        return edges, blocks

    def setup_copies():
        def sems(i):
            return ssend_sem.at[i], srecv_sem.at[i]

        return [
            (above1, below1, csend.at[1], crecv.at[0], sems(0), d + 1),
            (below1, above1, csend.at[0], crecv.at[1], sems(1), d - 1),
            (above1, below1, csn, crc.at[0], sems(2), d + 1),
            (below1, above1, csn, crc.at[1], sems(3), d - 1),
        ]

    def start(copies):
        for cond, _, src, dst, sems, other in copies:
            @pl.when(cond)
            def _():
                remote(src, dst, sems, other).start()

    def wait_recv(copies):
        for _, cond, src, dst, sems, other in copies:
            @pl.when(cond)
            def _():
                remote(src, dst, sems, other).wait_recv()

    def wait_send(copies):
        for cond, _, src, dst, sems, other in copies:
            @pl.when(cond)
            def _():
                remote(src, dst, sems, other).wait_send()

    def project(a):
        g = dot(gmat[...], vb[a])
        gb[a] = g.astype(BF16)
        c32[...] = g[GHOST:LO]

    project(0)

    pl.semaphore_wait(
        barrier,
        (ROW + ny + nz - 3) + below1.astype(jnp.int32) + below2.astype(jnp.int32)
        + above1.astype(jnp.int32) + above2.astype(jnp.int32),
    )
    for group in app_copies(0):
        start(group)
    start(setup_copies())

    fmat[:, GHOST:3 * GHOST] = rim[:, rims:].T.astype(BF16)
    place(pl.ds(rims, OWN))
    first, second = pl.ds(rims, 256), pl.ds(rims + 256, 256)
    cross = dot_nt(tcat[first, :], scat[second, :])
    amat[0:256, 256:] = cross.astype(BF16)
    amat[256:, 0:256] = cross.T.astype(BF16)

    def diagonal(block, q):
        rounded = block.astype(BF16)
        rows = pl.ds(q * GHOST, GHOST)
        amat[rows, rows] = rounded
        left = jnp.sum(jnp.where(eye, block - rounded.astype(F32), 0.0), axis=1, keepdims=True)
        dtab[rows, :] = jnp.broadcast_to(left, (GHOST, COLS))

    for half, rows in ((0, first), (1, second)):
        block = dot_nt(tcat[rows, :], scat[rows, :])
        at = half * 256
        amat[at:at + GHOST, at + GHOST:at + 256] = block[0:GHOST, GHOST:].astype(BF16)
        amat[at + GHOST:at + 256, at:at + GHOST] = block[GHOST:, 0:GHOST].astype(BF16)
        if half == 0:
            corner[0] = block[0:GHOST, 0:GHOST]
            diagonal(block[GHOST:, GHOST:], 1)
        else:
            diagonal(block[0:GHOST, 0:GHOST], 2)
            corner[1] = block[GHOST:, GHOST:]

    wait_recv(setup_copies())
    fmat[0:GHOST, 0:GHOST] = crecv[0, 0:GHOST, 0:GHOST]
    fmat[OWN - GHOST:, 3 * GHOST:4 * GHOST] = crecv[1, 0:GHOST, GHOST:]
    for side in range(2):
        at = (1 - side) * GHOST
        left = crecv[side, GHOST:, 0:GHOST].astype(F32)[0:1]
        block = corner[side] + crecv[side, 0:GHOST, at:at + GHOST].astype(F32) + jnp.where(eye, left, 0.0)
        diagonal(block, 3 * side)
    empty = jnp.zeros((ATOM_HOME * SLOT, 128), F32)
    for k, block in ((0, crc[0]), (1, csn[...]), (2, crc[1])):
        wide = jnp.concatenate([block, empty], axis=1)
        call[pl.ds(k * ATOM_HOME * SLOT, ATOM_HOME * SLOT), :] = wide if k == 0 else pltpu.roll(wide, k * HOME, axis=1)
    couple = call[...]
    couple_hi = couple.astype(BF16)
    couple_lo = (couple - couple_hi.astype(F32)).astype(BF16)
    fmat[:, OWN:] = (dot_tn(pall[...], couple_hi) + dot_tn(pall[...], couple_lo)).astype(BF16)

    half_width = (upper_edge - cut_edge) / 2.0
    centre = (upper_edge + cut_edge) / 2.0
    sigma_one = half_width / (lower_edge - centre)
    gamma_ratio = 2.0 / sigma_one
    sigma_two = 1.0 / (gamma_ratio - sigma_one)
    sigma_three = 1.0 / (gamma_ratio - sigma_two)
    scales = (sigma_one / half_width, 2.0 * sigma_two / half_width, 2.0 * sigma_three / half_width)
    backs = (0.0, sigma_one * sigma_two, sigma_two * sigma_three)

    for a in range(3):
        edges, blocks = app_copies(a)
        if a > 0:
            start(edges)
            project(a)
            start(blocks)
        acc[...] = dot(amat[...], vb[a]) + (dtab[...] * vb[a].astype(F32) - centre * fv[a])
        wait_recv(edges)
        acc[...] += dot(fmat[:, 0:OWN], xb[a, 0:OWN, :])
        wait_recv(blocks)
        below, above = rblk[a, 0].astype(F32), rblk[a, 1].astype(F32)
        own = c32[...]
        xb[a, OWN:OWN + HOME, :] = (own[0:HOME] + below[0:HOME] + rc2[a, 0].astype(F32)).astype(BF16)
        xb[a, OWN + HOME:OWN + 2 * HOME, :] = (
            own[HOME:2 * HOME] + below[HOME:2 * HOME] + above[GHOST:GHOST + HOME]
        ).astype(BF16)
        xb[a, OWN + 2 * HOME:OWN + 3 * HOME, :] = (
            own[2 * HOME:] + above[GHOST + HOME:] + rc2[a, 1].astype(F32)
        ).astype(BF16)
        acc[0:GHOST, :] += below[2 * HOME:]
        acc[OWN - GHOST:, :] += above[0:GHOST]
        new = (acc[...] + dot(fmat[:, OWN:], xb[a, OWN:, :])) * scales[a]
        if a > 0:
            new = new - backs[a] * fv[a - 1]
        fv[a + 1] = new
        if a < 2:
            vb[a + 1] = new.astype(BF16)

    result = fv.at[3]
    store = pltpu.make_async_copy(result, out_ref, out_sem)
    store.start()

    mine = jnp.sum(fv[3] * fv[3], axis=0, keepdims=True)
    base, sent = 0, []
    for (size, peer, me), sums in zip(stages, (part, ysum, zsum)):
        sums[me] = mine
        for k in far_first(size):
            copy = pltpu.make_async_remote_copy(
                src_ref=sums.at[me], dst_ref=sums.at[me],
                send_sem=nsend.at[base + k], recv_sem=nrecv.at[base + me],
                device_id=peer(k)[1], device_id_type=MESH,
            )
            copy.start()
            sent.append(copy)
        if base == 0:
            for a in range(3):
                for group in app_copies(a):
                    wait_send(group)
            wait_send(setup_copies())
        else:
            for copy in sent:
                copy.wait_send()
            sent = []
        for k in reversed(far_first(size)):
            i, where = peer(k)
            pltpu.make_async_remote_copy(
                src_ref=sums.at[i], dst_ref=sums.at[i],
                send_sem=nsend.at[base + k], recv_sem=nrecv.at[base + i],
                device_id=where, device_id_type=MESH,
            ).wait_recv()
        terms = [sums[i] for i in range(size)]
        while len(terms) > 1:
            terms = [sum(terms[i:i + 2][1:], terms[i]) for i in range(0, len(terms), 2)]
        mine = terms[0]
        base += size
    norm_ref[0, 0] = jnp.sqrt(jnp.sum(mine, axis=1, keepdims=True))[0, 0]

    store.wait()


def solution(mesh):
    ny = mesh.shape["wf"] // PLANE
    members = ROW + ny + ZLO * PLANE

    def local(wavefunctions, cell_matrix, cell_nodes, home_counts, atom_start, projectors, coupling):
        hbm = pl.BlockSpec(memory_space=pl.ANY)
        vmem = pl.BlockSpec(memory_space=pltpu.VMEM)
        smem = pl.BlockSpec(memory_space=pltpu.SMEM)
        filtered, norm = pl.pallas_call(
            functools.partial(kernel, ny),
            out_shape=(
                jax.ShapeDtypeStruct((OWN, COLS), F32),
                jax.ShapeDtypeStruct((1, 1), F32),
            ),
            in_specs=[hbm, hbm, vmem, smem, smem, hbm, hbm],
            out_specs=(hbm, smem),
            scratch_shapes=[
                pltpu.VMEM((4, OWN, COLS), F32),
                pltpu.VMEM((3, OWN, COLS), BF16),
                pltpu.VMEM((3, GROWS, COLS), BF16),
                pltpu.VMEM((3, EXT, COLS), BF16),
                pltpu.VMEM((3, 2, BLK, COLS), BF16),
                pltpu.VMEM((3, 2, HOME, COLS), BF16),
                pltpu.VMEM((PROWS, COLS), F32),
                pltpu.VMEM((OWN, COLS), F32),
                pltpu.VMEM((CELLS, NPC, NPC), BF16),
                pltpu.VMEM((EXT, CELLS * NPC), BF16),
                pltpu.VMEM((EXT, CELLS * NPC), BF16),
                pltpu.VMEM((GROWS, OWN), BF16),
                pltpu.VMEM((OWN, OWN), BF16),
                pltpu.VMEM((OWN, COLS), F32),
                pltpu.VMEM((OWN, EXT), BF16),
                pltpu.VMEM((2, GHOST, GHOST), F32),
                pltpu.VMEM((2, GHOST + 16, 2 * GHOST), BF16),
                pltpu.VMEM((2, GHOST + 16, 2 * GHOST), BF16),
                pltpu.VMEM((1, 3, NPROJ, ATOM_HOME, SUP), BF16),
                pltpu.VMEM((3 * ATOM_HOME * SLOT, OWN), F32),
                pltpu.VMEM((3 * ATOM_HOME * SLOT, OWN), BF16),
                pltpu.VMEM((NPROJ, ATOM_HOME, NPROJ), F32),
                pltpu.VMEM((ATOM_HOME * SLOT, 128), F32),
                pltpu.VMEM((ATOM_HOME * SLOT, 128), F32),
                pltpu.VMEM((2, ATOM_HOME * SLOT, 128), F32),
                pltpu.VMEM((3 * ATOM_HOME * SLOT, 256), F32),
                pltpu.VMEM((ROW, 1, COLS), F32),
                pltpu.VMEM((ny, 1, COLS), F32),
                pltpu.VMEM((ZLO * PLANE, 1, COLS), F32),
                pltpu.SemaphoreType.DMA((4,)),
                pltpu.SemaphoreType.DMA,
                pltpu.SemaphoreType.DMA((3, 8)),
                pltpu.SemaphoreType.DMA((3, 8)),
                pltpu.SemaphoreType.DMA((4,)),
                pltpu.SemaphoreType.DMA((4,)),
                pltpu.SemaphoreType.DMA((members,)),
                pltpu.SemaphoreType.DMA((members,)),
            ],
            compiler_params=pltpu.CompilerParams(collective_id=0, has_side_effects=True),
            name="chebyshev",
        )(
            wavefunctions, cell_matrix, cell_nodes, home_counts, atom_start.transpose(1, 0, 2),
            projectors.transpose(0, 1, 3, 2, 4), coupling.transpose(1, 0, 2),
        )
        return filtered, norm.reshape(())

    return jax.shard_map(
        local,
        mesh=mesh,
        in_specs=(
            P("dom", "wf"),
            P("dom", None, None),
            P("dom", None),
            P("dom", None),
            P("dom", None, None),
            P("dom", None, None, None, None),
            P("dom", None, None),
        ),
        out_specs=(P("dom", "wf"), P()),
        check_vma=False,
    )
```

```python
import functools

import jax
import jax.numpy as jnp
from jax import lax
from jax.experimental import pallas as pl
from jax.experimental.pallas import tpu as pltpu
from jax.sharding import PartitionSpec as P

F32, BF16 = jnp.float32, jnp.bfloat16
MESH = pl.DeviceIdType.MESH

lower_edge = -1.0
cut_edge = 2.0
upper_edge = 9.0

CELLS = 2
NPC = 512
OWN = 512
GHOST = 128
EXT = OWN + 2 * GHOST
COLS = 128
NPROJ, SUP, ATOM_HOME = 18, 256, 4
SLOT = 24
HOME = 80
PROWS = 3 * HOME
GROWS = 2 * GHOST + PROWS
BLK = GHOST + 2 * HOME
LO = GHOST + PROWS
ROW, PLANE, ZLO = 8, 3, 4


def dot(a, b):
    return jnp.dot(a, b, preferred_element_type=F32)


def dot_nt(a, b):
    return lax.dot_general(a, b, (((1,), (1,)), ((), ())), preferred_element_type=F32)


def dot_tn(a, b):
    return lax.dot_general(a, b, (((0,), (0,)), ((), ())), preferred_element_type=F32)


def kernel(
    ny,
    wave_ref, matrix_ref, nodes_hbm, counts_hbm, starts_hbm, proj_ref, coupling_ref,
    out_ref, norm_ref,
    fv, vb, gb, xb, rblk, rc2, c32, acc,
    cm, scat, tcat, gmat, amat, dtab, fmat, corner, csend, crecv,
    nodes_ref, counts_ref, starts_ref, pin, pst, pall, cin, cst, csn, crc, call,
    part, zsum,
    in_sem, send_sem, recv_sem, ssend_sem, srecv_sem,
    nsend, nrecv,
):
    d, w = lax.axis_index("dom"), lax.axis_index("wf")
    n_dom = 32
    below1, below2, above1, above2 = d >= 1, d >= 2, d < n_dom - 1, d < n_dom - 2

    loads = [
        pltpu.make_async_copy(proj_ref, pin, in_sem.at[0]),
        pltpu.make_async_copy(coupling_ref, cin, in_sem.at[1]),
        pltpu.make_async_copy(matrix_ref, cm, in_sem.at[2]),
        pltpu.make_async_copy(wave_ref, fv.at[0], in_sem.at[3]),
        pltpu.make_async_copy(nodes_hbm, nodes_ref, in_sem.at[4]),
        pltpu.make_async_copy(counts_hbm, counts_ref, in_sem.at[5]),
        pltpu.make_async_copy(starts_hbm, starts_ref, in_sem.at[6]),
    ]
    for i in (4, 5, 6, 0, 3, 2, 1):
        loads[i].start()

    zlo, row = lax.div(d, ROW), lax.rem(d, ROW)
    y, zhi = lax.div(w, PLANE), lax.rem(w, PLANE)
    z = zhi * ZLO + zlo
    nz = ZLO * PLANE

    def around(i, size):
        return i - size * (i >= size).astype(jnp.int32)

    def far_first(peers):
        return [p[1:] for p in sorted(peers, key=lambda p: -p[0])]

    def short(k, size):
        return min(k, size - k)

    plane = []
    for j in range(ny):
        for k in range(ROW):
            if j or k:
                yj, rk = around(y + j, ny), around(row + k, ROW)
                plane.append((short(j, ny) + short(k, ROW) / 2, yj * ROW + rk, (zlo * ROW + rk, yj * PLANE + zhi)))
    column = []
    for k in range(1, nz):
        i = around(z + k, nz)
        hi = (i >= ZLO).astype(jnp.int32) + (i >= 2 * ZLO).astype(jnp.int32)
        column.append((short(k, nz), i, ((i - ZLO * hi) * ROW + row, y * PLANE + hi)))
    stages = ((far_first(plane), y * ROW + row), (far_first(column), z))

    barrier = pltpu.get_barrier_semaphore()
    for cond, other in ((below1, d - 1), (above1, d + 1), (below2, d - 2), (above2, d + 2)):
        @pl.when(cond)
        def _():
            pl.semaphore_signal(barrier, inc=1, device_id=(other, w), device_id_type=MESH)
    for peers, _ in stages:
        for _, where in peers:
            pl.semaphore_signal(barrier, inc=1, device_id=where, device_id_type=MESH)

    def zero(ref):
        ref[...] = jnp.zeros(ref.shape, ref.dtype)

    for a in range(3):
        zero(xb.at[a, pl.ds(OWN, EXT - OWN)])
    for cond, part1, part2 in ((below1, 0, 0), (above1, 1, 1)):
        @pl.when(jnp.logical_not(cond))
        def _():
            for a in range(3):
                zero(rblk.at[a, part1])
                zero(xb.at[a, pl.ds(part2 * GHOST, GHOST)])
            zero(crecv.at[part1])
            zero(crc.at[part1])
    for cond, part1, part2 in ((below2, 0, 2), (above2, 1, 3)):
        @pl.when(jnp.logical_not(cond))
        def _():
            for a in range(3):
                zero(rc2.at[a, part1])
                zero(xb.at[a, pl.ds(part2 * GHOST, GHOST)])
    zero(pst)
    zero(cst)

    loads[4].wait()
    for c in range(CELLS):
        nodes = nodes_ref[pl.ds(c, 1), :]
        nodes = jnp.where(nodes < GHOST, nodes, jnp.where(nodes >= GHOST + OWN, nodes - OWN, nodes + GHOST))
        rows = lax.broadcasted_iota(jnp.int32, (EXT, NPC), 0)
        scat[:, c * NPC:(c + 1) * NPC] = jnp.where(rows == nodes, 1.0, 0.0).astype(BF16)

    loads[5].wait()
    loads[6].wait()
    loads[0].wait()
    for k in range(3):
        for j in range(ATOM_HOME):
            i = (k * ATOM_HOME + j) * SLOT
            pst[pl.ds(i, NPROJ), pl.ds(0, SUP)] = pin[0, k, :, j, :].astype(F32)
            live = jnp.where(j < counts_ref[0, k], 1.0, 0.0).astype(F32)
            placed = pltpu.roll(pst[pl.ds(i, SLOT), :], starts_ref[k, 0, j], axis=1)
            pst[pl.ds(i, SLOT), :] = placed * live
    pall[...] = pst[...].astype(BF16)
    col = lax.broadcasted_iota(jnp.int32, (1, 3 * ATOM_HOME * SLOT), 1)
    slot, p = lax.div(col, SLOT), lax.rem(col, SLOT)
    target = lax.div(slot, ATOM_HOME) * HOME + lax.rem(slot, ATOM_HOME) * NPROJ + p
    target = jnp.where(p < NPROJ, target, -1)
    pick = jnp.where(
        lax.broadcasted_iota(jnp.int32, (PROWS, 3 * ATOM_HOME * SLOT), 0) == target, 1.0, 0.0
    ).astype(BF16)
    gmat[pl.ds(GHOST, PROWS), :] = dot(pick, pall[...]).astype(BF16)

    loads[1].wait()
    for j in range(ATOM_HOME):
        cst[pl.ds(j * SLOT, NPROJ), pl.ds(0, NPROJ)] = cin[:, j, :]
        rows = cst[pl.ds(j * SLOT, SLOT), :]
        csn[pl.ds(j * SLOT, SLOT), :] = rows if j == 0 else pltpu.roll(rows, j * NPROJ, axis=1)

    even = lax.rem(d, 2) == 0
    odd = jnp.logical_not(even)

    def both(*conds):
        return functools.reduce(jnp.logical_and, conds)

    def remote(src, dst, sems, other):
        return pltpu.make_async_remote_copy(
            src_ref=src, dst_ref=dst, send_sem=sems[0], recv_sem=sems[1],
            device_id=(other, w), device_id_type=MESH,
        )

    def app_copies(a):
        def sems(i, j=None):
            return send_sem.at[a, i if j is None else j], recv_sem.at[a, i]

        low, high = vb.at[a, pl.ds(0, GHOST)], vb.at[a, pl.ds(OWN - GHOST, GHOST)]

        def x(i):
            return xb.at[a, pl.ds(i * GHOST, GHOST)]

        def g(start, rows):
            return gb.at[a, pl.ds(start, rows)]

        near = [
            (above1, below1, high, x(0), sems(0), d + 1),
            (below1, above1, low, x(1), sems(1), d - 1),
        ]
        far = [
            (both(even, above2), below2, high, x(2), sems(2), d + 2),
            (both(odd, below2), above2, low, x(3), sems(3), d - 2),
        ]
        relay = [
            (both(even, below1), None, x(0), x(2), sems(2, 10), d + 1),
            (both(odd, above1), None, x(1), x(3), sems(3, 11), d - 1),
        ]
        coefs = [
            (above1, below1, g(GHOST + HOME, 2 * HOME), rblk.at[a, 0, pl.ds(0, 2 * HOME)], sems(4), d + 1),
            (below1, above1, g(GHOST, 2 * HOME), rblk.at[a, 1, pl.ds(GHOST, 2 * HOME)], sems(5), d - 1),
            (above2, below2, g(GHOST + 2 * HOME, HOME), rc2.at[a, 0], sems(6), d + 2),
            (below2, above2, g(GHOST, HOME), rc2.at[a, 1], sems(7), d - 2),
        ]
        rim_sums = [
            (above1, below1, g(LO, GHOST), rblk.at[a, 0, pl.ds(2 * HOME, GHOST)], sems(8), d + 1),
            (below1, above1, g(0, GHOST), rblk.at[a, 1, pl.ds(0, GHOST)], sems(9), d - 1),
        ]
        return near, far, relay, coefs, rim_sums

    def setup_copies():
        def sems(i):
            return ssend_sem.at[i], srecv_sem.at[i]

        corners = [
            (above1, below1, csend.at[1], crecv.at[0], sems(0), d + 1),
            (below1, above1, csend.at[0], crecv.at[1], sems(1), d - 1),
        ]
        couplings = [
            (above1, below1, csn, crc.at[0], sems(2), d + 1),
            (below1, above1, csn, crc.at[1], sems(3), d - 1),
        ]
        return corners, couplings

    def start(copies):
        for cond, _, src, dst, sems, other in copies:
            @pl.when(cond)
            def _():
                remote(src, dst, sems, other).start()

    def wait_recv(copies):
        for _, cond, src, dst, sems, other in copies:
            @pl.when(cond)
            def _():
                remote(src, dst, sems, other).wait_recv()

    def wait_send(copies):
        for cond, _, src, dst, sems, other in copies:
            @pl.when(cond)
            def _():
                remote(src, dst, sems, other).wait_send()

    def project(a):
        coefs = dot(gmat[GHOST:LO, :], vb[a])
        gb[a, GHOST:LO, :] = coefs.astype(BF16)
        c32[...] = coefs

    def sum_rims(a):
        gb[a, 0:GHOST, :] = dot(gmat[0:GHOST, :], vb[a]).astype(BF16)
        gb[a, LO:, :] = dot(gmat[LO:, :], vb[a]).astype(BF16)

    loads[3].wait()
    vb[0] = fv[0].astype(BF16)
    project(0)
    pl.semaphore_wait(
        barrier,
        sum(len(peers) for peers, _ in stages) + below1.astype(jnp.int32) + below2.astype(jnp.int32)
        + above1.astype(jnp.int32) + above2.astype(jnp.int32),
    )
    for i in (0, 1, 3):
        start(app_copies(0)[i])
    start(setup_copies()[1])

    loads[2].wait()

    rims = 2 * GHOST
    eye = lax.broadcasted_iota(jnp.int32, (GHOST, GHOST), 0) == lax.broadcasted_iota(jnp.int32, (GHOST, GHOST), 1)

    def place(rows):
        for c in range(CELLS):
            cell = pl.ds(c * NPC, NPC)
            tcat[rows, cell] = dot(scat[rows, cell], cm[c]).astype(BF16)

    place(pl.ds(0, rims))
    rim = dot_nt(tcat[0:rims, :], scat[...])
    gmat[pl.ds(0, GHOST), :] = rim[0:GHOST, rims:].astype(BF16)
    gmat[pl.ds(LO, GHOST), :] = rim[GHOST:, rims:].astype(BF16)
    for side in range(2):
        ends = rim[side * GHOST:(side + 1) * GHOST, 0:rims]
        rounded = ends.astype(BF16)
        csend[side, 0:GHOST, :] = rounded
        left = (ends - rounded.astype(F32))[:, side * GHOST:(side + 1) * GHOST]
        left = jnp.sum(jnp.where(eye, left, 0.0), axis=0, keepdims=True)
        csend[side, GHOST:, 0:GHOST] = jnp.broadcast_to(left, (16, GHOST)).astype(BF16)

    near, far, relay, coefs, rim_sums = app_copies(0)
    corners, couplings = setup_copies()
    sum_rims(0)
    start(rim_sums)
    start(corners)
    wait_recv(near)
    start(relay)

    fmat[:, 0:rims] = rim[:, rims:].T.astype(BF16)
    place(pl.ds(rims, OWN))
    first, second = pl.ds(rims, 256), pl.ds(rims + 256, 256)
    cross = dot_nt(tcat[first, :], scat[second, :])
    amat[0:256, 256:] = cross.astype(BF16)
    amat[256:, 0:256] = cross.T.astype(BF16)

    def diagonal(block, q):
        rounded = block.astype(BF16)
        rows = pl.ds(q * GHOST, GHOST)
        amat[rows, rows] = rounded
        left = jnp.sum(jnp.where(eye, block - rounded.astype(F32), 0.0), axis=1, keepdims=True)
        dtab[rows, :] = jnp.broadcast_to(left, (GHOST, COLS))

    for half, rows in ((0, first), (1, second)):
        block = dot_nt(tcat[rows, :], scat[rows, :])
        at = half * 256
        amat[at:at + GHOST, at + GHOST:at + 256] = block[0:GHOST, GHOST:].astype(BF16)
        amat[at + GHOST:at + 256, at:at + GHOST] = block[GHOST:, 0:GHOST].astype(BF16)
        if half == 0:
            corner[0] = block[0:GHOST, 0:GHOST]
            diagonal(block[GHOST:, GHOST:], 1)
        else:
            diagonal(block[0:GHOST, 0:GHOST], 2)
            corner[1] = block[GHOST:, GHOST:]

    wait_recv(couplings)
    wait_recv(corners)
    for side in range(2):
        at = (1 - side) * GHOST
        left = crecv[side, GHOST:, 0:GHOST].astype(F32)[0:1]
        block = corner[side] + crecv[side, 0:GHOST, at:at + GHOST].astype(F32) + jnp.where(eye, left, 0.0)
        diagonal(block, 3 * side)
    empty = jnp.zeros((ATOM_HOME * SLOT, 128), F32)
    for k, block in ((0, crc[0]), (1, csn[...]), (2, crc[1])):
        wide = jnp.concatenate([block, empty], axis=1)
        call[pl.ds(k * ATOM_HOME * SLOT, ATOM_HOME * SLOT), :] = wide if k == 0 else pltpu.roll(wide, k * HOME, axis=1)
    couple = call[...]
    couple_hi = couple.astype(BF16)
    couple_lo = (couple - couple_hi.astype(F32)).astype(BF16)
    fmat[:, rims:] = (dot_tn(pall[...], couple_hi) + dot_tn(pall[...], couple_lo)).astype(BF16)

    half_width = (upper_edge - cut_edge) / 2.0
    centre = (upper_edge + cut_edge) / 2.0
    sigma_one = half_width / (lower_edge - centre)
    gamma_ratio = 2.0 / sigma_one
    sigma_two = 1.0 / (gamma_ratio - sigma_one)
    sigma_three = 1.0 / (gamma_ratio - sigma_two)
    scales = (sigma_one / half_width, 2.0 * sigma_two / half_width, 2.0 * sigma_three / half_width)
    backs = (0.0, sigma_one * sigma_two, sigma_two * sigma_three)

    for a in range(3):
        near, far, relay, coefs, rim_sums = app_copies(a)
        if a > 0:
            start(near)
            start(far)
            project(a)
            start(coefs)
            sum_rims(a)
            start(rim_sums)
        acc[...] = dot(amat[...], vb[a]) + (dtab[...] * vb[a].astype(F32) - centre * fv[a])
        if a > 0:
            wait_recv(near)
            start(relay)
        acc[...] += dot(fmat[:, 0:rims], xb[a, 0:rims, :])
        wait_recv(coefs)
        below, above = rblk[a, 0, 0:2 * HOME, :].astype(F32), rblk[a, 1, GHOST:, :].astype(F32)
        own = c32[...]
        xb[a, OWN:OWN + HOME, :] = (own[0:HOME] + below[0:HOME] + rc2[a, 0].astype(F32)).astype(BF16)
        xb[a, OWN + HOME:OWN + 2 * HOME, :] = (
            own[HOME:2 * HOME] + below[HOME:2 * HOME] + above[0:HOME]
        ).astype(BF16)
        xb[a, OWN + 2 * HOME:OWN + 3 * HOME, :] = (
            own[2 * HOME:] + above[HOME:] + rc2[a, 1].astype(F32)
        ).astype(BF16)
        acc[...] += dot(fmat[:, rims:], xb[a, OWN:, :])
        wait_recv(far)
        wait_recv(rim_sums)
        acc[0:GHOST, :] += rblk[a, 0, 2 * HOME:, :].astype(F32) + dot(
            crecv[0, 0:GHOST, 0:GHOST], xb[a, 2 * GHOST:3 * GHOST, :]
        )
        acc[OWN - GHOST:, :] += rblk[a, 1, 0:GHOST, :].astype(F32) + dot(
            crecv[1, 0:GHOST, GHOST:], xb[a, 3 * GHOST:4 * GHOST, :]
        )
        new = acc[...] * scales[a]
        if a > 0:
            new = new - backs[a] * fv[a - 1]
        if a == 2:
            out_ref[...] = new
        else:
            fv[a + 1] = new
            vb[a + 1] = new.astype(BF16)

    mine = jnp.sum(new * new, axis=0, keepdims=True)
    base, sent = 0, []
    for (peers, me), sums in zip(stages, (part, zsum)):
        sums[me] = mine
        for k, (_, where) in enumerate(peers):
            copy = pltpu.make_async_remote_copy(
                src_ref=sums.at[me], dst_ref=sums.at[me],
                send_sem=nsend.at[base + k], recv_sem=nrecv.at[base + me],
                device_id=where, device_id_type=MESH,
            )
            copy.start()
            sent.append(copy)
        if base == 0:
            for a in range(3):
                for group in app_copies(a):
                    wait_send(group)
            for group in setup_copies():
                wait_send(group)
        else:
            for copy in sent:
                copy.wait_send()
        for k, (i, where) in reversed(list(enumerate(peers))):
            pltpu.make_async_remote_copy(
                src_ref=sums.at[i], dst_ref=sums.at[i],
                send_sem=nsend.at[base + k], recv_sem=nrecv.at[base + i],
                device_id=where, device_id_type=MESH,
            ).wait_recv()
        size = len(peers) + 1
        terms = [sums[i] for i in range(size)]
        while len(terms) > 1:
            terms = [sum(terms[i:i + 2][1:], terms[i]) for i in range(0, len(terms), 2)]
        mine = terms[0]
        base += size
    norm_ref[0, 0] = jnp.sqrt(jnp.sum(mine, axis=1, keepdims=True))[0, 0]


def solution(mesh):
    ny = mesh.shape["wf"] // PLANE
    members = ROW * ny + ZLO * PLANE

    def local(wavefunctions, cell_matrix, cell_nodes, home_counts, atom_start, projectors, coupling):
        hbm = pl.BlockSpec(memory_space=pl.ANY)
        vmem = pl.BlockSpec(memory_space=pltpu.VMEM)
        smem = pl.BlockSpec(memory_space=pltpu.SMEM)
        filtered, norm = pl.pallas_call(
            functools.partial(kernel, ny),
            out_shape=(
                pltpu.VMEM((OWN, COLS), F32),
                jax.ShapeDtypeStruct((1, 1), F32),
            ),
            in_specs=[hbm] * 7,
            out_specs=(vmem, smem),
            scratch_shapes=[
                pltpu.VMEM((4, OWN, COLS), F32),
                pltpu.VMEM((3, OWN, COLS), BF16),
                pltpu.VMEM((3, GROWS, COLS), BF16),
                pltpu.VMEM((3, EXT, COLS), BF16),
                pltpu.VMEM((3, 2, BLK, COLS), BF16),
                pltpu.VMEM((3, 2, HOME, COLS), BF16),
                pltpu.VMEM((PROWS, COLS), F32),
                pltpu.VMEM((OWN, COLS), F32),
                pltpu.VMEM((CELLS, NPC, NPC), BF16),
                pltpu.VMEM((EXT, CELLS * NPC), BF16),
                pltpu.VMEM((EXT, CELLS * NPC), BF16),
                pltpu.VMEM((GROWS, OWN), BF16),
                pltpu.VMEM((OWN, OWN), BF16),
                pltpu.VMEM((OWN, COLS), F32),
                pltpu.VMEM((OWN, 2 * GHOST + 256), BF16),
                pltpu.VMEM((2, GHOST, GHOST), F32),
                pltpu.VMEM((2, GHOST + 16, 2 * GHOST), BF16),
                pltpu.VMEM((2, GHOST + 16, 2 * GHOST), BF16),
                pltpu.VMEM((CELLS, NPC), jnp.int32),
                pltpu.SMEM((1, 3), jnp.int32),
                pltpu.SMEM((3, 1, ATOM_HOME), jnp.int32),
                pltpu.VMEM((1, 3, NPROJ, ATOM_HOME, SUP), BF16),
                pltpu.VMEM((3 * ATOM_HOME * SLOT, OWN), F32),
                pltpu.VMEM((3 * ATOM_HOME * SLOT, OWN), BF16),
                pltpu.VMEM((NPROJ, ATOM_HOME, NPROJ), F32),
                pltpu.VMEM((ATOM_HOME * SLOT, 128), F32),
                pltpu.VMEM((ATOM_HOME * SLOT, 128), F32),
                pltpu.VMEM((2, ATOM_HOME * SLOT, 128), F32),
                pltpu.VMEM((3 * ATOM_HOME * SLOT, 256), F32),
                pltpu.VMEM((ROW * ny, 1, COLS), F32),
                pltpu.VMEM((ZLO * PLANE, 1, COLS), F32),
                pltpu.SemaphoreType.DMA((7,)),
                pltpu.SemaphoreType.DMA((3, 12)),
                pltpu.SemaphoreType.DMA((3, 10)),
                pltpu.SemaphoreType.DMA((4,)),
                pltpu.SemaphoreType.DMA((4,)),
                pltpu.SemaphoreType.DMA((members,)),
                pltpu.SemaphoreType.DMA((members,)),
            ],
            compiler_params=pltpu.CompilerParams(collective_id=0, has_side_effects=True),
            name="chebyshev",
        )(
            wavefunctions, cell_matrix, cell_nodes, home_counts, atom_start.transpose(1, 0, 2),
            projectors.transpose(0, 1, 3, 2, 4), coupling.transpose(1, 0, 2),
        )
        return filtered, norm.reshape(())

    return jax.shard_map(
        local,
        mesh=mesh,
        in_specs=(
            P("dom", "wf"),
            P("dom", None, None),
            P("dom", None),
            P("dom", None),
            P("dom", None, None),
            P("dom", None, None, None, None),
            P("dom", None, None),
        ),
        out_specs=(P("dom", "wf"), P()),
        check_vma=False,
    )
```

```python
import functools

import jax
import jax.numpy as jnp
from jax import lax
from jax.experimental import pallas as pl
from jax.experimental.pallas import tpu as pltpu
from jax.sharding import PartitionSpec as P

F32, BF16 = jnp.float32, jnp.bfloat16
MESH = pl.DeviceIdType.MESH

lower_edge = -1.0
cut_edge = 2.0
upper_edge = 9.0

CELLS = 2
NPC = 512
OWN = 512
GHOST = 128
EXT = OWN + 2 * GHOST
COLS = 128
NPROJ, SUP, ATOM_HOME = 18, 256, 4
SLOT = 24
HOME = 80
PROWS = 3 * HOME
GROWS = 2 * GHOST + PROWS
BLK = GHOST + 2 * HOME
LO = GHOST + PROWS
ROW, PLANE, ZLO = 8, 3, 4


def dot(a, b):
    return jnp.dot(a, b, preferred_element_type=F32)


def dot_nt(a, b):
    return lax.dot_general(a, b, (((1,), (1,)), ((), ())), preferred_element_type=F32)


def dot_tn(a, b):
    return lax.dot_general(a, b, (((0,), (0,)), ((), ())), preferred_element_type=F32)


def kernel(
    ny,
    wave_ref, matrix_ref, nodes_hbm, counts_hbm, starts_hbm, proj_ref, coupling_ref,
    out_ref, norm_ref,
    fv, vb, gb, xb, rblk, rc2, c32, acc,
    cm, scat, tcat, gmat, amat, dtab, fmat, corner, csend, crecv,
    nodes_ref, counts_ref, starts_ref, pin, pst, pall, cin, cst, csn, crc, call,
    part, zsum,
    in_sem, send_sem, recv_sem, ssend_sem, srecv_sem,
    nsend, nrecv, token,
):
    d, w = lax.axis_index("dom"), lax.axis_index("wf")
    n_dom = 32
    below1, below2, above1, above2 = d >= 1, d >= 2, d < n_dom - 1, d < n_dom - 2

    loads = [
        pltpu.make_async_copy(proj_ref, pin, in_sem.at[0]),
        pltpu.make_async_copy(coupling_ref, cin, in_sem.at[1]),
        pltpu.make_async_copy(matrix_ref, cm, in_sem.at[2]),
        pltpu.make_async_copy(wave_ref, fv.at[0], in_sem.at[3]),
        pltpu.make_async_copy(nodes_hbm, nodes_ref, in_sem.at[4]),
        pltpu.make_async_copy(counts_hbm, counts_ref, in_sem.at[5]),
        pltpu.make_async_copy(starts_hbm, starts_ref, in_sem.at[6]),
    ]
    for i in (4, 5, 6, 0, 3, 2, 1):
        loads[i].start()

    zlo, row = lax.div(d, ROW), lax.rem(d, ROW)
    y, zhi = lax.div(w, PLANE), lax.rem(w, PLANE)
    z = zhi * ZLO + zlo
    nz = ZLO * PLANE

    def around(i, size):
        return i - size * (i >= size).astype(jnp.int32)

    def far_first(peers):
        return [p[1:] for p in sorted(peers, key=lambda p: -p[0])]

    def short(k, size):
        return min(k, size - k)

    plane = []
    for j in range(ny):
        for k in range(ROW):
            if j or k:
                yj, rk = around(y + j, ny), around(row + k, ROW)
                plane.append((short(j, ny) + short(k, ROW) / 2, yj * ROW + rk, (zlo * ROW + rk, yj * PLANE + zhi)))
    column = []
    for k in range(1, nz):
        i = around(z + k, nz)
        hi = (i >= ZLO).astype(jnp.int32) + (i >= 2 * ZLO).astype(jnp.int32)
        column.append((short(k, nz), i, ((i - ZLO * hi) * ROW + row, y * PLANE + hi)))
    stages = ((far_first(plane), y * ROW + row), (far_first(column), z))

    def ring(dy, dz):
        j, i = around(y + dy % ny, ny), around(z + dz % nz, nz)
        hi = (i >= ZLO).astype(jnp.int32) + (i >= 2 * ZLO).astype(jnp.int32)
        return (i - ZLO * hi) * ROW + row, j * PLANE + hi

    beside = [(zlo * ROW + around(row + k, ROW), w) for k in range(1, ROW)]
    next_ones = [ring(1, 0), ring(-1, 0), ring(0, 1), ring(0, -1)]
    beside = beside + next_ones
    tokens = [
        next_ones,
        [ring(2, 0), ring(-2, 0), ring(0, 2), ring(0, -2)],
        [ring(1, 0), ring(-1, 0), ring(0, 2), ring(0, -2)],
    ]

    def send_token(i):
        for where in tokens[i]:
            pl.semaphore_signal(token.at[i], inc=1, device_id=where, device_id_type=MESH)

    def wait_token(i):
        pl.semaphore_wait(token.at[i], len(tokens[i]))

    barrier = pltpu.get_barrier_semaphore()
    for cond, other in ((below1, d - 1), (above1, d + 1), (below2, d - 2), (above2, d + 2)):
        @pl.when(cond)
        def _():
            pl.semaphore_signal(barrier, inc=1, device_id=(other, w), device_id_type=MESH)
    for where in beside:
        pl.semaphore_signal(barrier, inc=1, device_id=where, device_id_type=MESH)

    def zero(ref):
        ref[...] = jnp.zeros(ref.shape, ref.dtype)

    for a in range(3):
        zero(xb.at[a, pl.ds(OWN, EXT - OWN)])
    for cond, part1, part2 in ((below1, 0, 0), (above1, 1, 1)):
        @pl.when(jnp.logical_not(cond))
        def _():
            for a in range(3):
                zero(rblk.at[a, part1])
                zero(xb.at[a, pl.ds(part2 * GHOST, GHOST)])
            zero(crecv.at[part1])
            zero(crc.at[part1])
    for cond, part1, part2 in ((below2, 0, 2), (above2, 1, 3)):
        @pl.when(jnp.logical_not(cond))
        def _():
            for a in range(3):
                zero(rc2.at[a, part1])
                zero(xb.at[a, pl.ds(part2 * GHOST, GHOST)])
    zero(pst)
    zero(cst)

    loads[4].wait()
    for c in range(CELLS):
        nodes = nodes_ref[pl.ds(c, 1), :]
        nodes = jnp.where(nodes < GHOST, nodes, jnp.where(nodes >= GHOST + OWN, nodes - OWN, nodes + GHOST))
        rows = lax.broadcasted_iota(jnp.int32, (EXT, NPC), 0)
        scat[:, c * NPC:(c + 1) * NPC] = jnp.where(rows == nodes, 1.0, 0.0).astype(BF16)

    loads[5].wait()
    loads[6].wait()
    loads[0].wait()
    for k in range(3):
        for j in range(ATOM_HOME):
            i = (k * ATOM_HOME + j) * SLOT
            pst[pl.ds(i, NPROJ), pl.ds(0, SUP)] = pin[0, k, :, j, :].astype(F32)
            live = jnp.where(j < counts_ref[0, k], 1.0, 0.0).astype(F32)
            placed = pltpu.roll(pst[pl.ds(i, SLOT), :], starts_ref[k, 0, j], axis=1)
            pst[pl.ds(i, SLOT), :] = placed * live
    pall[...] = pst[...].astype(BF16)
    col = lax.broadcasted_iota(jnp.int32, (1, 3 * ATOM_HOME * SLOT), 1)
    slot, p = lax.div(col, SLOT), lax.rem(col, SLOT)
    target = lax.div(slot, ATOM_HOME) * HOME + lax.rem(slot, ATOM_HOME) * NPROJ + p
    target = jnp.where(p < NPROJ, target, -1)
    pick = jnp.where(
        lax.broadcasted_iota(jnp.int32, (PROWS, 3 * ATOM_HOME * SLOT), 0) == target, 1.0, 0.0
    ).astype(BF16)
    gmat[pl.ds(GHOST, PROWS), :] = dot(pick, pall[...]).astype(BF16)

    loads[1].wait()
    for j in range(ATOM_HOME):
        cst[pl.ds(j * SLOT, NPROJ), pl.ds(0, NPROJ)] = cin[:, j, :]
        rows = cst[pl.ds(j * SLOT, SLOT), :]
        csn[pl.ds(j * SLOT, SLOT), :] = rows if j == 0 else pltpu.roll(rows, j * NPROJ, axis=1)

    even = lax.rem(d, 2) == 0
    odd = jnp.logical_not(even)

    def both(*conds):
        return functools.reduce(jnp.logical_and, conds)

    def remote(src, dst, sems, other):
        return pltpu.make_async_remote_copy(
            src_ref=src, dst_ref=dst, send_sem=sems[0], recv_sem=sems[1],
            device_id=(other, w), device_id_type=MESH,
        )

    def app_copies(a):
        def sems(i, j=None):
            return send_sem.at[a, i if j is None else j], recv_sem.at[a, i]

        low, high = vb.at[a, pl.ds(0, GHOST)], vb.at[a, pl.ds(OWN - GHOST, GHOST)]

        def x(i):
            return xb.at[a, pl.ds(i * GHOST, GHOST)]

        def g(start, rows):
            return gb.at[a, pl.ds(start, rows)]

        near = [
            (above1, below1, high, x(0), sems(0), d + 1),
            (below1, above1, low, x(1), sems(1), d - 1),
        ]
        far = [
            (both(even, above2), below2, high, x(2), sems(2), d + 2),
            (both(odd, below2), above2, low, x(3), sems(3), d - 2),
        ]
        relay = [
            (both(even, below1), None, x(0), x(2), sems(2, 10), d + 1),
            (both(odd, above1), None, x(1), x(3), sems(3, 11), d - 1),
        ]
        coefs = [
            (above1, below1, g(GHOST + HOME, 2 * HOME), rblk.at[a, 0, pl.ds(0, 2 * HOME)], sems(4), d + 1),
            (below1, above1, g(GHOST, 2 * HOME), rblk.at[a, 1, pl.ds(GHOST, 2 * HOME)], sems(5), d - 1),
            (above2, below2, g(GHOST + 2 * HOME, HOME), rc2.at[a, 0], sems(6), d + 2),
            (below2, above2, g(GHOST, HOME), rc2.at[a, 1], sems(7), d - 2),
        ]
        rim_sums = [
            (above1, below1, g(LO, GHOST), rblk.at[a, 0, pl.ds(2 * HOME, GHOST)], sems(8), d + 1),
            (below1, above1, g(0, GHOST), rblk.at[a, 1, pl.ds(0, GHOST)], sems(9), d - 1),
        ]
        return near, far, relay, coefs, rim_sums

    def setup_copies():
        def sems(i):
            return ssend_sem.at[i], srecv_sem.at[i]

        corners = [
            (above1, below1, csend.at[1], crecv.at[0], sems(0), d + 1),
            (below1, above1, csend.at[0], crecv.at[1], sems(1), d - 1),
        ]
        couplings = [
            (above1, below1, csn, crc.at[0], sems(2), d + 1),
            (below1, above1, csn, crc.at[1], sems(3), d - 1),
        ]
        return corners, couplings

    def start(copies):
        for cond, _, src, dst, sems, other in copies:
            @pl.when(cond)
            def _():
                remote(src, dst, sems, other).start()

    def wait_recv(copies):
        for _, cond, src, dst, sems, other in copies:
            @pl.when(cond)
            def _():
                remote(src, dst, sems, other).wait_recv()

    def wait_send(copies):
        for cond, _, src, dst, sems, other in copies:
            @pl.when(cond)
            def _():
                remote(src, dst, sems, other).wait_send()

    def project(a):
        coefs = dot(gmat[GHOST:LO, :], vb[a])
        gb[a, GHOST:LO, :] = coefs.astype(BF16)
        c32[...] = coefs

    def sum_rims(a):
        gb[a, 0:GHOST, :] = dot(gmat[0:GHOST, :], vb[a]).astype(BF16)
        gb[a, LO:, :] = dot(gmat[LO:, :], vb[a]).astype(BF16)

    loads[3].wait()
    vb[0] = fv[0].astype(BF16)
    project(0)
    pl.semaphore_wait(
        barrier,
        len(beside) + below1.astype(jnp.int32) + below2.astype(jnp.int32)
        + above1.astype(jnp.int32) + above2.astype(jnp.int32),
    )
    for i in (0, 1, 3):
        start(app_copies(0)[i])
    start(setup_copies()[1])
    send_token(0)

    loads[2].wait()

    rims = 2 * GHOST
    eye = lax.broadcasted_iota(jnp.int32, (GHOST, GHOST), 0) == lax.broadcasted_iota(jnp.int32, (GHOST, GHOST), 1)

    def place(rows):
        for c in range(CELLS):
            cell = pl.ds(c * NPC, NPC)
            tcat[rows, cell] = dot(scat[rows, cell], cm[c]).astype(BF16)

    place(pl.ds(0, rims))
    rim = dot_nt(tcat[0:rims, :], scat[...])
    gmat[pl.ds(0, GHOST), :] = rim[0:GHOST, rims:].astype(BF16)
    gmat[pl.ds(LO, GHOST), :] = rim[GHOST:, rims:].astype(BF16)
    for side in range(2):
        ends = rim[side * GHOST:(side + 1) * GHOST, 0:rims]
        rounded = ends.astype(BF16)
        csend[side, 0:GHOST, :] = rounded
        left = (ends - rounded.astype(F32))[:, side * GHOST:(side + 1) * GHOST]
        left = jnp.sum(jnp.where(eye, left, 0.0), axis=0, keepdims=True)
        csend[side, GHOST:, 0:GHOST] = jnp.broadcast_to(left, (16, GHOST)).astype(BF16)

    near, far, relay, coefs, rim_sums = app_copies(0)
    corners, couplings = setup_copies()
    sum_rims(0)
    start(rim_sums)
    start(corners)
    wait_recv(near)
    start(relay)

    fmat[:, 0:rims] = rim[:, rims:].T.astype(BF16)
    place(pl.ds(rims, OWN))
    first, second = pl.ds(rims, 256), pl.ds(rims + 256, 256)
    cross = dot_nt(tcat[first, :], scat[second, :])
    amat[0:256, 256:] = cross.astype(BF16)
    amat[256:, 0:256] = cross.T.astype(BF16)

    def diagonal(block, q):
        rounded = block.astype(BF16)
        rows = pl.ds(q * GHOST, GHOST)
        amat[rows, rows] = rounded
        left = jnp.sum(jnp.where(eye, block - rounded.astype(F32), 0.0), axis=1, keepdims=True)
        dtab[rows, :] = jnp.broadcast_to(left, (GHOST, COLS))

    for half, rows in ((0, first), (1, second)):
        block = dot_nt(tcat[rows, :], scat[rows, :])
        at = half * 256
        amat[at:at + GHOST, at + GHOST:at + 256] = block[0:GHOST, GHOST:].astype(BF16)
        amat[at + GHOST:at + 256, at:at + GHOST] = block[GHOST:, 0:GHOST].astype(BF16)
        if half == 0:
            corner[0] = block[0:GHOST, 0:GHOST]
            diagonal(block[GHOST:, GHOST:], 1)
        else:
            diagonal(block[0:GHOST, 0:GHOST], 2)
            corner[1] = block[GHOST:, GHOST:]

    wait_recv(couplings)
    wait_recv(corners)
    wait_token(0)
    send_token(1)
    for side in range(2):
        at = (1 - side) * GHOST
        left = crecv[side, GHOST:, 0:GHOST].astype(F32)[0:1]
        block = corner[side] + crecv[side, 0:GHOST, at:at + GHOST].astype(F32) + jnp.where(eye, left, 0.0)
        diagonal(block, 3 * side)
    empty = jnp.zeros((ATOM_HOME * SLOT, 128), F32)
    for k, block in ((0, crc[0]), (1, csn[...]), (2, crc[1])):
        wide = jnp.concatenate([block, empty], axis=1)
        call[pl.ds(k * ATOM_HOME * SLOT, ATOM_HOME * SLOT), :] = wide if k == 0 else pltpu.roll(wide, k * HOME, axis=1)
    couple = call[...]
    couple_hi = couple.astype(BF16)
    couple_lo = (couple - couple_hi.astype(F32)).astype(BF16)
    fmat[:, rims:] = (dot_tn(pall[...], couple_hi) + dot_tn(pall[...], couple_lo)).astype(BF16)

    half_width = (upper_edge - cut_edge) / 2.0
    centre = (upper_edge + cut_edge) / 2.0
    sigma_one = half_width / (lower_edge - centre)
    gamma_ratio = 2.0 / sigma_one
    sigma_two = 1.0 / (gamma_ratio - sigma_one)
    sigma_three = 1.0 / (gamma_ratio - sigma_two)
    scales = (sigma_one / half_width, 2.0 * sigma_two / half_width, 2.0 * sigma_three / half_width)
    backs = (0.0, sigma_one * sigma_two, sigma_two * sigma_three)

    for a in range(3):
        near, far, relay, coefs, rim_sums = app_copies(a)
        if a > 0:
            start(near)
            start(far)
            project(a)
            start(coefs)
            sum_rims(a)
            start(rim_sums)
            wait_token(a)
            if a == 1:
                send_token(2)
        acc[...] = dot(amat[...], vb[a]) + (dtab[...] * vb[a].astype(F32) - centre * fv[a])
        if a > 0:
            wait_recv(near)
            start(relay)
        acc[...] += dot(fmat[:, 0:rims], xb[a, 0:rims, :])
        wait_recv(coefs)
        below, above = rblk[a, 0, 0:2 * HOME, :].astype(F32), rblk[a, 1, GHOST:, :].astype(F32)
        own = c32[...]
        xb[a, OWN:OWN + HOME, :] = (own[0:HOME] + below[0:HOME] + rc2[a, 0].astype(F32)).astype(BF16)
        xb[a, OWN + HOME:OWN + 2 * HOME, :] = (
            own[HOME:2 * HOME] + below[HOME:2 * HOME] + above[0:HOME]
        ).astype(BF16)
        xb[a, OWN + 2 * HOME:OWN + 3 * HOME, :] = (
            own[2 * HOME:] + above[HOME:] + rc2[a, 1].astype(F32)
        ).astype(BF16)
        acc[...] += dot(fmat[:, rims:], xb[a, OWN:, :])
        wait_recv(far)
        wait_recv(rim_sums)
        acc[0:GHOST, :] += rblk[a, 0, 2 * HOME:, :].astype(F32) + dot(
            crecv[0, 0:GHOST, 0:GHOST], xb[a, 2 * GHOST:3 * GHOST, :]
        )
        acc[OWN - GHOST:, :] += rblk[a, 1, 0:GHOST, :].astype(F32) + dot(
            crecv[1, 0:GHOST, GHOST:], xb[a, 3 * GHOST:4 * GHOST, :]
        )
        new = acc[...] * scales[a]
        if a > 0:
            new = new - backs[a] * fv[a - 1]
        if a == 2:
            out_ref[...] = new
        else:
            fv[a + 1] = new
            vb[a + 1] = new.astype(BF16)

    mine = jnp.sum(new * new, axis=0, keepdims=True)
    base, sent = 0, []
    for (peers, me), sums in zip(stages, (part, zsum)):
        sums[me] = mine
        for k, (_, where) in enumerate(peers):
            copy = pltpu.make_async_remote_copy(
                src_ref=sums.at[me], dst_ref=sums.at[me],
                send_sem=nsend.at[base + k], recv_sem=nrecv.at[base + me],
                device_id=where, device_id_type=MESH,
            )
            copy.start()
            sent.append(copy)
        if base == 0:
            for a in range(3):
                for group in app_copies(a):
                    wait_send(group)
            for group in setup_copies():
                wait_send(group)
        else:
            for copy in sent:
                copy.wait_send()
        for k, (i, where) in reversed(list(enumerate(peers))):
            pltpu.make_async_remote_copy(
                src_ref=sums.at[i], dst_ref=sums.at[i],
                send_sem=nsend.at[base + k], recv_sem=nrecv.at[base + i],
                device_id=where, device_id_type=MESH,
            ).wait_recv()
        size = len(peers) + 1
        terms = [sums[i] for i in range(size)]
        while len(terms) > 1:
            terms = [sum(terms[i:i + 2][1:], terms[i]) for i in range(0, len(terms), 2)]
        mine = terms[0]
        base += size
    norm_ref[0, 0] = jnp.sqrt(jnp.sum(mine, axis=1, keepdims=True))[0, 0]


def solution(mesh):
    ny = mesh.shape["wf"] // PLANE
    members = ROW * ny + ZLO * PLANE

    def local(wavefunctions, cell_matrix, cell_nodes, home_counts, atom_start, projectors, coupling):
        hbm = pl.BlockSpec(memory_space=pl.ANY)
        vmem = pl.BlockSpec(memory_space=pltpu.VMEM)
        smem = pl.BlockSpec(memory_space=pltpu.SMEM)
        filtered, norm = pl.pallas_call(
            functools.partial(kernel, ny),
            out_shape=(
                pltpu.VMEM((OWN, COLS), F32),
                jax.ShapeDtypeStruct((1, 1), F32),
            ),
            in_specs=[hbm] * 7,
            out_specs=(vmem, smem),
            scratch_shapes=[
                pltpu.VMEM((4, OWN, COLS), F32),
                pltpu.VMEM((3, OWN, COLS), BF16),
                pltpu.VMEM((3, GROWS, COLS), BF16),
                pltpu.VMEM((3, EXT, COLS), BF16),
                pltpu.VMEM((3, 2, BLK, COLS), BF16),
                pltpu.VMEM((3, 2, HOME, COLS), BF16),
                pltpu.VMEM((PROWS, COLS), F32),
                pltpu.VMEM((OWN, COLS), F32),
                pltpu.VMEM((CELLS, NPC, NPC), BF16),
                pltpu.VMEM((EXT, CELLS * NPC), BF16),
                pltpu.VMEM((EXT, CELLS * NPC), BF16),
                pltpu.VMEM((GROWS, OWN), BF16),
                pltpu.VMEM((OWN, OWN), BF16),
                pltpu.VMEM((OWN, COLS), F32),
                pltpu.VMEM((OWN, 2 * GHOST + 256), BF16),
                pltpu.VMEM((2, GHOST, GHOST), F32),
                pltpu.VMEM((2, GHOST + 16, 2 * GHOST), BF16),
                pltpu.VMEM((2, GHOST + 16, 2 * GHOST), BF16),
                pltpu.VMEM((CELLS, NPC), jnp.int32),
                pltpu.SMEM((1, 3), jnp.int32),
                pltpu.SMEM((3, 1, ATOM_HOME), jnp.int32),
                pltpu.VMEM((1, 3, NPROJ, ATOM_HOME, SUP), BF16),
                pltpu.VMEM((3 * ATOM_HOME * SLOT, OWN), F32),
                pltpu.VMEM((3 * ATOM_HOME * SLOT, OWN), BF16),
                pltpu.VMEM((NPROJ, ATOM_HOME, NPROJ), F32),
                pltpu.VMEM((ATOM_HOME * SLOT, 128), F32),
                pltpu.VMEM((ATOM_HOME * SLOT, 128), F32),
                pltpu.VMEM((2, ATOM_HOME * SLOT, 128), F32),
                pltpu.VMEM((3 * ATOM_HOME * SLOT, 256), F32),
                pltpu.VMEM((ROW * ny, 1, COLS), F32),
                pltpu.VMEM((ZLO * PLANE, 1, COLS), F32),
                pltpu.SemaphoreType.DMA((7,)),
                pltpu.SemaphoreType.DMA((3, 12)),
                pltpu.SemaphoreType.DMA((3, 10)),
                pltpu.SemaphoreType.DMA((4,)),
                pltpu.SemaphoreType.DMA((4,)),
                pltpu.SemaphoreType.DMA((members,)),
                pltpu.SemaphoreType.DMA((members,)),
                pltpu.SemaphoreType.REGULAR((3,)),
            ],
            compiler_params=pltpu.CompilerParams(collective_id=0, has_side_effects=True),
            name="chebyshev",
        )(
            wavefunctions, cell_matrix, cell_nodes, home_counts, atom_start.transpose(1, 0, 2),
            projectors.transpose(0, 1, 3, 2, 4), coupling.transpose(1, 0, 2),
        )
        return filtered, norm.reshape(())

    return jax.shard_map(
        local,
        mesh=mesh,
        in_specs=(
            P("dom", "wf"),
            P("dom", None, None),
            P("dom", None),
            P("dom", None),
            P("dom", None, None),
            P("dom", None, None, None, None),
            P("dom", None, None),
        ),
        out_specs=(P("dom", "wf"), P()),
        check_vma=False,
    )
```

```python
import functools

import jax
import jax.numpy as jnp
from jax import lax
from jax.experimental import pallas as pl
from jax.experimental.pallas import tpu as pltpu
from jax.sharding import PartitionSpec as P

F32, BF16 = jnp.float32, jnp.bfloat16
MESH = pl.DeviceIdType.MESH

lower_edge = -1.0
cut_edge = 2.0
upper_edge = 9.0

CELLS = 2
NPC = 512
OWN = 512
GHOST = 128
EXT = OWN + 2 * GHOST
COLS = 128
NPROJ, SUP, ATOM_HOME = 18, 256, 4
SLOT = 24
HOME = 72
PROWS = 3 * HOME
GROWS = 2 * GHOST + PROWS
BLK = GHOST + 2 * HOME
LO = GHOST + PROWS
ROW, PLANE, ZLO = 8, 3, 4


def dot(a, b):
    return jnp.dot(a, b, preferred_element_type=F32)


def dot_nt(a, b):
    return lax.dot_general(a, b, (((1,), (1,)), ((), ())), preferred_element_type=F32)


def dot_tn(a, b):
    return lax.dot_general(a, b, (((0,), (0,)), ((), ())), preferred_element_type=F32)


def kernel(
    ny,
    wave_ref, matrix_ref, nodes_hbm, counts_hbm, starts_hbm, proj_ref, coupling_ref,
    out_ref, norm_ref,
    fv, vb, gb, xb, rblk, rc2, c32, acc,
    cm, scat, tcat, gmat, amat, dtab, fmat, corner, csend, crecv,
    nodes_ref, counts_ref, starts_ref, pin, pst, pall, cin, cst, csn, crc, call,
    part, zsum,
    in_sem, send_sem, recv_sem, ssend_sem, srecv_sem,
    nsend, nrecv, token,
):
    d, w = lax.axis_index("dom"), lax.axis_index("wf")
    n_dom = 32
    below1, below2, above1, above2 = d >= 1, d >= 2, d < n_dom - 1, d < n_dom - 2

    loads = [
        pltpu.make_async_copy(proj_ref, pin, in_sem.at[0]),
        pltpu.make_async_copy(coupling_ref, cin, in_sem.at[1]),
        pltpu.make_async_copy(matrix_ref, cm, in_sem.at[2]),
        pltpu.make_async_copy(wave_ref, fv.at[0], in_sem.at[3]),
        pltpu.make_async_copy(nodes_hbm, nodes_ref, in_sem.at[4]),
        pltpu.make_async_copy(counts_hbm, counts_ref, in_sem.at[5]),
        pltpu.make_async_copy(starts_hbm, starts_ref, in_sem.at[6]),
    ]
    for i in (4, 5, 6, 0, 3, 2, 1):
        loads[i].start()

    zlo, row = lax.div(d, ROW), lax.rem(d, ROW)
    y, zhi = lax.div(w, PLANE), lax.rem(w, PLANE)
    z = zhi * ZLO + zlo
    nz = ZLO * PLANE

    def around(i, size):
        return i - size * (i >= size).astype(jnp.int32)

    def far_first(peers):
        return [p[1:] for p in sorted(peers, key=lambda p: -p[0])]

    def short(k, size):
        return min(k, size - k)

    plane = []
    for j in range(ny):
        for k in range(ROW):
            if j or k:
                yj, rk = around(y + j, ny), around(row + k, ROW)
                plane.append((short(j, ny) + short(k, ROW) / 2, yj * ROW + rk, (zlo * ROW + rk, yj * PLANE + zhi)))
    column = []
    for k in range(1, nz):
        i = around(z + k, nz)
        hi = (i >= ZLO).astype(jnp.int32) + (i >= 2 * ZLO).astype(jnp.int32)
        column.append((short(k, nz), i, ((i - ZLO * hi) * ROW + row, y * PLANE + hi)))
    stages = ((far_first(plane), y * ROW + row), (far_first(column), z))

    def ring(dy, dz):
        j, i = around(y + dy % ny, ny), around(z + dz % nz, nz)
        hi = (i >= ZLO).astype(jnp.int32) + (i >= 2 * ZLO).astype(jnp.int32)
        return (i - ZLO * hi) * ROW + row, j * PLANE + hi

    beside = [(zlo * ROW + around(row + k, ROW), w) for k in range(1, ROW)]
    next_ones = [ring(1, 0), ring(-1, 0), ring(0, 1), ring(0, -1)]
    beside = beside + next_ones
    tokens = [
        next_ones,
        [ring(2, 0), ring(-2, 0), ring(0, 2), ring(0, -2)],
        [ring(1, 0), ring(-1, 0), ring(0, 2), ring(0, -2)],
    ]

    def send_token(i):
        for where in tokens[i]:
            pl.semaphore_signal(token.at[i], inc=1, device_id=where, device_id_type=MESH)

    def wait_token(i):
        pl.semaphore_wait(token.at[i], len(tokens[i]))

    barrier = pltpu.get_barrier_semaphore()
    for cond, other in ((below1, d - 1), (above1, d + 1), (below2, d - 2), (above2, d + 2)):
        @pl.when(cond)
        def _():
            pl.semaphore_signal(barrier, inc=1, device_id=(other, w), device_id_type=MESH)
    for where in beside:
        pl.semaphore_signal(barrier, inc=1, device_id=where, device_id_type=MESH)

    def zero(ref):
        ref[...] = jnp.zeros(ref.shape, ref.dtype)

    for a in range(3):
        zero(xb.at[a, pl.ds(OWN, EXT - OWN)])
    for cond, part1, part2 in ((below1, 0, 0), (above1, 1, 1)):
        @pl.when(jnp.logical_not(cond))
        def _():
            for a in range(3):
                zero(rblk.at[a, part1])
                zero(xb.at[a, pl.ds(part2 * GHOST, GHOST)])
            zero(crecv.at[part1])
            zero(crc.at[part1])
    even = lax.rem(d, 2) == 0
    odd = jnp.logical_not(even)
    for cond, passed, part1, part2 in ((below2, odd, 0, 2), (above2, even, 1, 3)):
        @pl.when(jnp.logical_not(cond))
        def _():
            for a in range(3):
                zero(rc2.at[a, part1])

        @pl.when(jnp.logical_not(jnp.logical_and(cond, passed)))
        def _():
            for a in range(3):
                zero(xb.at[a, pl.ds(part2 * GHOST, GHOST)])
    zero(pst)
    zero(cst)

    loads[4].wait()
    for c in range(CELLS):
        nodes = nodes_ref[pl.ds(c, 1), :]
        nodes = jnp.where(nodes < GHOST, nodes, jnp.where(nodes >= GHOST + OWN, nodes - OWN, nodes + GHOST))
        rows = lax.broadcasted_iota(jnp.int32, (EXT, NPC), 0)
        scat[:, c * NPC:(c + 1) * NPC] = jnp.where(rows == nodes, 1.0, 0.0).astype(BF16)

    loads[5].wait()
    loads[6].wait()
    loads[0].wait()
    for k in range(3):
        for j in range(ATOM_HOME):
            i = (k * ATOM_HOME + j) * SLOT
            pst[pl.ds(i, NPROJ), pl.ds(0, SUP)] = pin[0, k, :, j, :].astype(F32)
            live = jnp.where(j < counts_ref[0, k], 1.0, 0.0).astype(F32)
            placed = pltpu.roll(pst[pl.ds(i, SLOT), :], starts_ref[k, 0, j], axis=1)
            pst[pl.ds(i, SLOT), :] = placed * live
    pall[...] = pst[...].astype(BF16)
    col = lax.broadcasted_iota(jnp.int32, (1, 3 * ATOM_HOME * SLOT), 1)
    slot, p = lax.div(col, SLOT), lax.rem(col, SLOT)
    target = lax.div(slot, ATOM_HOME) * HOME + lax.rem(slot, ATOM_HOME) * NPROJ + p
    target = jnp.where(p < NPROJ, target, -1)
    pick = jnp.where(
        lax.broadcasted_iota(jnp.int32, (PROWS, 3 * ATOM_HOME * SLOT), 0) == target, 1.0, 0.0
    ).astype(BF16)
    gmat[pl.ds(GHOST, PROWS), :] = dot(pick, pall[...]).astype(BF16)

    loads[1].wait()
    for j in range(ATOM_HOME):
        cst[pl.ds(j * SLOT, NPROJ), pl.ds(0, NPROJ)] = cin[:, j, :]
        rows = cst[pl.ds(j * SLOT, SLOT), :]
        csn[pl.ds(j * SLOT, SLOT), :] = rows if j == 0 else pltpu.roll(rows, j * NPROJ, axis=1)

    def both(*conds):
        return functools.reduce(jnp.logical_and, conds)

    def remote(src, dst, sems, other):
        return pltpu.make_async_remote_copy(
            src_ref=src, dst_ref=dst, send_sem=sems[0], recv_sem=sems[1],
            device_id=(other, w), device_id_type=MESH,
        )

    def app_copies(a):
        def sems(i, j=None):
            return send_sem.at[a, i if j is None else j], recv_sem.at[a, i]

        low, high = vb.at[a, pl.ds(0, GHOST)], vb.at[a, pl.ds(OWN - GHOST, GHOST)]

        def x(i):
            return xb.at[a, pl.ds(i * GHOST, GHOST)]

        def g(start, rows):
            return gb.at[a, pl.ds(start, rows)]

        near = [
            (above1, below1, high, x(0), sems(0), d + 1),
            (below1, above1, low, x(1), sems(1), d - 1),
        ]
        relay = [
            (both(even, below1), both(odd, below2), x(0), x(2), sems(2, 10), d + 1),
            (both(odd, above1), both(even, above2), x(1), x(3), sems(3, 11), d - 1),
        ]
        coefs = [
            (above1, below1, g(GHOST + HOME, 2 * HOME), rblk.at[a, 0, pl.ds(0, 2 * HOME)], sems(4), d + 1),
            (below1, above1, g(GHOST, 2 * HOME), rblk.at[a, 1, pl.ds(GHOST, 2 * HOME)], sems(5), d - 1),
            (above2, below2, g(GHOST + 2 * HOME, HOME), rc2.at[a, 0], sems(6), d + 2),
            (below2, above2, g(GHOST, HOME), rc2.at[a, 1], sems(7), d - 2),
        ]
        rim_sums = [
            (above1, below1, g(LO, GHOST), rblk.at[a, 0, pl.ds(2 * HOME, GHOST)], sems(8), d + 1),
            (below1, above1, g(0, GHOST), rblk.at[a, 1, pl.ds(0, GHOST)], sems(9), d - 1),
        ]
        return near, relay, coefs, rim_sums

    def setup_copies():
        def sems(i):
            return ssend_sem.at[i], srecv_sem.at[i]

        corners = [
            (above1, below1, csend.at[1], crecv.at[0], sems(0), d + 1),
            (below1, above1, csend.at[0], crecv.at[1], sems(1), d - 1),
        ]
        couplings = [
            (above1, below1, csn, crc.at[0], sems(2), d + 1),
            (below1, above1, csn, crc.at[1], sems(3), d - 1),
        ]
        return corners, couplings

    def start(copies):
        for cond, _, src, dst, sems, other in copies:
            @pl.when(cond)
            def _():
                remote(src, dst, sems, other).start()

    def wait_recv(copies):
        for _, cond, src, dst, sems, other in copies:
            @pl.when(cond)
            def _():
                remote(src, dst, sems, other).wait_recv()

    def wait_send(copies):
        for cond, _, src, dst, sems, other in copies:
            @pl.when(cond)
            def _():
                remote(src, dst, sems, other).wait_send()

    def project(a):
        coefs = dot(gmat[GHOST:LO, :], vb[a])
        gb[a, GHOST:LO, :] = coefs.astype(BF16)
        c32[...] = coefs

    def sum_rims(a, near):
        low, high = dot(gmat[0:GHOST, :], vb[a]), dot(gmat[LO:, :], vb[a])

        @pl.when(odd)
        def _():
            wait_recv(near[0:1])
            gb[a, 0:GHOST, :] = low.astype(BF16)
            gb[a, LO:, :] = (high + dot(csend[1, 0:GHOST, 0:GHOST], xb[a, 0:GHOST, :])).astype(BF16)

        @pl.when(even)
        def _():
            wait_recv(near[1:2])
            gb[a, 0:GHOST, :] = (low + dot(csend[0, 0:GHOST, GHOST:], xb[a, GHOST:2 * GHOST, :])).astype(BF16)
            gb[a, LO:, :] = high.astype(BF16)

    def wait_linked(near):
        @pl.when(odd)
        def _():
            wait_recv(near[1:2])

        @pl.when(even)
        def _():
            wait_recv(near[0:1])

    loads[3].wait()
    vb[0] = fv[0].astype(BF16)
    project(0)
    pl.semaphore_wait(
        barrier,
        len(beside) + below1.astype(jnp.int32) + below2.astype(jnp.int32)
        + above1.astype(jnp.int32) + above2.astype(jnp.int32),
    )
    for i in (0, 2):
        start(app_copies(0)[i])
    start(setup_copies()[1])
    send_token(0)

    loads[2].wait()

    rims = 2 * GHOST
    eye = lax.broadcasted_iota(jnp.int32, (GHOST, GHOST), 0) == lax.broadcasted_iota(jnp.int32, (GHOST, GHOST), 1)

    def place(rows):
        for c in range(CELLS):
            cell = pl.ds(c * NPC, NPC)
            tcat[rows, cell] = dot(scat[rows, cell], cm[c]).astype(BF16)

    place(pl.ds(0, rims))
    rim = dot_nt(tcat[0:rims, :], scat[...])
    gmat[pl.ds(0, GHOST), :] = rim[0:GHOST, rims:].astype(BF16)
    gmat[pl.ds(LO, GHOST), :] = rim[GHOST:, rims:].astype(BF16)
    for side in range(2):
        ends = rim[side * GHOST:(side + 1) * GHOST, 0:rims]
        rounded = ends.astype(BF16)
        csend[side, 0:GHOST, :] = rounded
        left = (ends - rounded.astype(F32))[:, side * GHOST:(side + 1) * GHOST]
        left = jnp.sum(jnp.where(eye, left, 0.0), axis=0, keepdims=True)
        csend[side, GHOST:, 0:GHOST] = jnp.broadcast_to(left, (16, GHOST)).astype(BF16)

    near, relay, coefs, rim_sums = app_copies(0)
    corners, couplings = setup_copies()
    sum_rims(0, near)
    start(rim_sums)
    start(corners)
    wait_linked(near)
    start(relay)

    fmat[:, 0:rims] = rim[:, rims:].T.astype(BF16)
    place(pl.ds(rims, OWN))
    first, second = pl.ds(rims, 256), pl.ds(rims + 256, 256)
    cross = dot_nt(tcat[first, :], scat[second, :])
    amat[0:256, 256:] = cross.astype(BF16)
    amat[256:, 0:256] = cross.T.astype(BF16)

    def diagonal(block, q):
        rounded = block.astype(BF16)
        rows = pl.ds(q * GHOST, GHOST)
        amat[rows, rows] = rounded
        left = jnp.sum(jnp.where(eye, block - rounded.astype(F32), 0.0), axis=1, keepdims=True)
        dtab[rows, :] = jnp.broadcast_to(left, (GHOST, COLS))

    for half, rows in ((0, first), (1, second)):
        block = dot_nt(tcat[rows, :], scat[rows, :])
        at = half * 256
        amat[at:at + GHOST, at + GHOST:at + 256] = block[0:GHOST, GHOST:].astype(BF16)
        amat[at + GHOST:at + 256, at:at + GHOST] = block[GHOST:, 0:GHOST].astype(BF16)
        if half == 0:
            corner[0] = block[0:GHOST, 0:GHOST]
            diagonal(block[GHOST:, GHOST:], 1)
        else:
            diagonal(block[0:GHOST, 0:GHOST], 2)
            corner[1] = block[GHOST:, GHOST:]

    wait_recv(couplings)
    wait_recv(corners)
    wait_token(0)
    send_token(1)
    for side in range(2):
        at = (1 - side) * GHOST
        left = crecv[side, GHOST:, 0:GHOST].astype(F32)[0:1]
        block = corner[side] + crecv[side, 0:GHOST, at:at + GHOST].astype(F32) + jnp.where(eye, left, 0.0)
        diagonal(block, 3 * side)
    empty = jnp.zeros((ATOM_HOME * SLOT, 128), F32)
    for k, block in ((0, crc[0]), (1, csn[...]), (2, crc[1])):
        wide = jnp.concatenate([block, empty], axis=1)
        call[pl.ds(k * ATOM_HOME * SLOT, ATOM_HOME * SLOT), :] = wide if k == 0 else pltpu.roll(wide, k * HOME, axis=1)
    couple = call[...]
    couple_hi = couple.astype(BF16)
    couple_lo = (couple - couple_hi.astype(F32)).astype(BF16)
    fmat[:, rims:] = (dot_tn(pall[...], couple_hi) + dot_tn(pall[...], couple_lo)).astype(BF16)

    half_width = (upper_edge - cut_edge) / 2.0
    centre = (upper_edge + cut_edge) / 2.0
    sigma_one = half_width / (lower_edge - centre)
    gamma_ratio = 2.0 / sigma_one
    sigma_two = 1.0 / (gamma_ratio - sigma_one)
    sigma_three = 1.0 / (gamma_ratio - sigma_two)
    scales = (sigma_one / half_width, 2.0 * sigma_two / half_width, 2.0 * sigma_three / half_width)
    backs = (0.0, sigma_one * sigma_two, sigma_two * sigma_three)

    for a in range(3):
        near, relay, coefs, rim_sums = app_copies(a)
        if a > 0:
            start(near)
            project(a)
            start(coefs)
            sum_rims(a, near)
            start(rim_sums)
            wait_token(a)
            if a == 1:
                send_token(2)
        acc[...] = dot(amat[...], vb[a]) + (dtab[...] * vb[a].astype(F32) - centre * fv[a])
        if a > 0:
            wait_linked(near)
            start(relay)
        acc[...] += dot(fmat[:, 0:rims], xb[a, 0:rims, :])
        wait_recv(coefs)
        below, above = rblk[a, 0, 0:2 * HOME, :].astype(F32), rblk[a, 1, GHOST:, :].astype(F32)
        own = c32[...]
        xb[a, OWN:OWN + HOME, :] = (own[0:HOME] + below[0:HOME] + rc2[a, 0].astype(F32)).astype(BF16)
        xb[a, OWN + HOME:OWN + 2 * HOME, :] = (
            own[HOME:2 * HOME] + below[HOME:2 * HOME] + above[0:HOME]
        ).astype(BF16)
        xb[a, OWN + 2 * HOME:OWN + 3 * HOME, :] = (
            own[2 * HOME:] + above[HOME:] + rc2[a, 1].astype(F32)
        ).astype(BF16)
        acc[...] += dot(fmat[:, rims:], xb[a, OWN:, :])
        wait_recv(relay)
        wait_recv(rim_sums)
        acc[0:GHOST, :] += rblk[a, 0, 2 * HOME:, :].astype(F32) + dot(
            crecv[0, 0:GHOST, 0:GHOST], xb[a, 2 * GHOST:3 * GHOST, :]
        )
        acc[OWN - GHOST:, :] += rblk[a, 1, 0:GHOST, :].astype(F32) + dot(
            crecv[1, 0:GHOST, GHOST:], xb[a, 3 * GHOST:4 * GHOST, :]
        )
        new = acc[...] * scales[a]
        if a > 0:
            new = new - backs[a] * fv[a - 1]
        if a == 2:
            out_ref[...] = new
        else:
            fv[a + 1] = new
            vb[a + 1] = new.astype(BF16)

    mine = jnp.sum(new * new, axis=0, keepdims=True)
    base, sent = 0, []
    for (peers, me), sums in zip(stages, (part, zsum)):
        sums[me] = mine
        for k, (_, where) in enumerate(peers):
            copy = pltpu.make_async_remote_copy(
                src_ref=sums.at[me], dst_ref=sums.at[me],
                send_sem=nsend.at[base + k], recv_sem=nrecv.at[base + me],
                device_id=where, device_id_type=MESH,
            )
            copy.start()
            sent.append(copy)
        if base == 0:
            for a in range(3):
                for group in app_copies(a):
                    wait_send(group)
            for group in setup_copies():
                wait_send(group)
        else:
            for copy in sent:
                copy.wait_send()
        for k, (i, where) in reversed(list(enumerate(peers))):
            pltpu.make_async_remote_copy(
                src_ref=sums.at[i], dst_ref=sums.at[i],
                send_sem=nsend.at[base + k], recv_sem=nrecv.at[base + i],
                device_id=where, device_id_type=MESH,
            ).wait_recv()
        size = len(peers) + 1
        terms = [sums[i] for i in range(size)]
        while len(terms) > 1:
            terms = [sum(terms[i:i + 2][1:], terms[i]) for i in range(0, len(terms), 2)]
        mine = terms[0]
        base += size
    norm_ref[0, 0] = jnp.sqrt(jnp.sum(mine, axis=1, keepdims=True))[0, 0]


def solution(mesh):
    ny = mesh.shape["wf"] // PLANE
    members = ROW * ny + ZLO * PLANE

    def local(wavefunctions, cell_matrix, cell_nodes, home_counts, atom_start, projectors, coupling):
        hbm = pl.BlockSpec(memory_space=pl.ANY)
        vmem = pl.BlockSpec(memory_space=pltpu.VMEM)
        smem = pl.BlockSpec(memory_space=pltpu.SMEM)
        filtered, norm = pl.pallas_call(
            functools.partial(kernel, ny),
            out_shape=(
                pltpu.VMEM((OWN, COLS), F32),
                jax.ShapeDtypeStruct((1, 1), F32),
            ),
            in_specs=[hbm] * 7,
            out_specs=(vmem, smem),
            scratch_shapes=[
                pltpu.VMEM((4, OWN, COLS), F32),
                pltpu.VMEM((3, OWN, COLS), BF16),
                pltpu.VMEM((3, GROWS, COLS), BF16),
                pltpu.VMEM((3, EXT, COLS), BF16),
                pltpu.VMEM((3, 2, BLK, COLS), BF16),
                pltpu.VMEM((3, 2, HOME, COLS), BF16),
                pltpu.VMEM((PROWS, COLS), F32),
                pltpu.VMEM((OWN, COLS), F32),
                pltpu.VMEM((CELLS, NPC, NPC), BF16),
                pltpu.VMEM((EXT, CELLS * NPC), BF16),
                pltpu.VMEM((EXT, CELLS * NPC), BF16),
                pltpu.VMEM((GROWS, OWN), BF16),
                pltpu.VMEM((OWN, OWN), BF16),
                pltpu.VMEM((OWN, COLS), F32),
                pltpu.VMEM((OWN, 2 * GHOST + 256), BF16),
                pltpu.VMEM((2, GHOST, GHOST), F32),
                pltpu.VMEM((2, GHOST + 16, 2 * GHOST), BF16),
                pltpu.VMEM((2, GHOST + 16, 2 * GHOST), BF16),
                pltpu.VMEM((CELLS, NPC), jnp.int32),
                pltpu.SMEM((1, 3), jnp.int32),
                pltpu.SMEM((3, 1, ATOM_HOME), jnp.int32),
                pltpu.VMEM((1, 3, NPROJ, ATOM_HOME, SUP), BF16),
                pltpu.VMEM((3 * ATOM_HOME * SLOT, OWN), F32),
                pltpu.VMEM((3 * ATOM_HOME * SLOT, OWN), BF16),
                pltpu.VMEM((NPROJ, ATOM_HOME, NPROJ), F32),
                pltpu.VMEM((ATOM_HOME * SLOT, 128), F32),
                pltpu.VMEM((ATOM_HOME * SLOT, 128), F32),
                pltpu.VMEM((2, ATOM_HOME * SLOT, 128), F32),
                pltpu.VMEM((3 * ATOM_HOME * SLOT, 256), F32),
                pltpu.VMEM((ROW * ny, 1, COLS), F32),
                pltpu.VMEM((ZLO * PLANE, 1, COLS), F32),
                pltpu.SemaphoreType.DMA((7,)),
                pltpu.SemaphoreType.DMA((3, 12)),
                pltpu.SemaphoreType.DMA((3, 10)),
                pltpu.SemaphoreType.DMA((4,)),
                pltpu.SemaphoreType.DMA((4,)),
                pltpu.SemaphoreType.DMA((members,)),
                pltpu.SemaphoreType.DMA((members,)),
                pltpu.SemaphoreType.REGULAR((3,)),
            ],
            compiler_params=pltpu.CompilerParams(collective_id=0, has_side_effects=True),
            name="chebyshev",
        )(
            wavefunctions, cell_matrix, cell_nodes, home_counts, atom_start.transpose(1, 0, 2),
            projectors.transpose(0, 1, 3, 2, 4), coupling.transpose(1, 0, 2),
        )
        return filtered, norm.reshape(())

    return jax.shard_map(
        local,
        mesh=mesh,
        in_specs=(
            P("dom", "wf"),
            P("dom", None, None),
            P("dom", None),
            P("dom", None),
            P("dom", None, None),
            P("dom", None, None, None, None),
            P("dom", None, None),
        ),
        out_specs=(P("dom", "wf"), P()),
        check_vma=False,
    )
```

```python
import functools

import jax
import jax.numpy as jnp
from jax import lax
from jax.experimental import pallas as pl
from jax.experimental.pallas import tpu as pltpu
from jax.sharding import PartitionSpec as P

F32, BF16 = jnp.float32, jnp.bfloat16
MESH = pl.DeviceIdType.MESH

lower_edge = -1.0
cut_edge = 2.0
upper_edge = 9.0

CELLS = 2
NPC = 512
OWN = 512
GHOST = 128
EXT = OWN + 2 * GHOST
COLS = 128
NPROJ, SUP, ATOM_HOME = 18, 256, 4
SLOT = 24
HOME = 72
PROWS = 3 * HOME
GROWS = 2 * GHOST + PROWS
BLK = GHOST + 2 * HOME
LO = GHOST + PROWS
ROW, PLANE, ZLO = 8, 3, 4


def dot(a, b):
    return jnp.dot(a, b, preferred_element_type=F32)


def dot_nt(a, b):
    return lax.dot_general(a, b, (((1,), (1,)), ((), ())), preferred_element_type=F32)


def dot_tn(a, b):
    return lax.dot_general(a, b, (((0,), (0,)), ((), ())), preferred_element_type=F32)


def kernel(
    ny,
    wave_ref, matrix_ref, nodes_hbm, counts_hbm, starts_hbm, proj_ref, coupling_ref,
    out_ref, norm_ref,
    fv, vb, gb, xb, rblk, rc2, c32, acc,
    cm, scat, tcat, gmat, amat, dtab, fmat, corner, csend, crecv,
    nodes_ref, counts_ref, starts_ref, pin, pst, pall, cin, cst, csn, crc, call,
    part, zsum,
    in_sem, send_sem, recv_sem, ssend_sem, srecv_sem,
    nsend, nrecv, token,
):
    d, w = lax.axis_index("dom"), lax.axis_index("wf")
    n_dom = 32
    below1, below2, above1, above2 = d >= 1, d >= 2, d < n_dom - 1, d < n_dom - 2

    loads = [
        pltpu.make_async_copy(proj_ref, pin, in_sem.at[0]),
        pltpu.make_async_copy(coupling_ref, cin, in_sem.at[1]),
        pltpu.make_async_copy(matrix_ref, cm, in_sem.at[2]),
        pltpu.make_async_copy(wave_ref, fv.at[0], in_sem.at[3]),
        pltpu.make_async_copy(nodes_hbm, nodes_ref, in_sem.at[4]),
        pltpu.make_async_copy(counts_hbm, counts_ref, in_sem.at[5]),
        pltpu.make_async_copy(starts_hbm, starts_ref, in_sem.at[6]),
    ]
    for i in (4, 5, 6, 0, 3, 2, 1):
        loads[i].start()

    zlo, row = lax.div(d, ROW), lax.rem(d, ROW)
    y, zhi = lax.div(w, PLANE), lax.rem(w, PLANE)
    z = zhi * ZLO + zlo
    nz = ZLO * PLANE

    def around(i, size):
        return i - size * (i >= size).astype(jnp.int32)

    def far_first(peers):
        return [p[1:] for p in sorted(peers, key=lambda p: -p[0])]

    def short(k, size):
        return min(k, size - k)

    plane = []
    for j in range(ny):
        for k in range(ROW):
            if j or k:
                yj, rk = around(y + j, ny), around(row + k, ROW)
                plane.append((short(j, ny) + short(k, ROW) / 2, yj * ROW + rk, (zlo * ROW + rk, yj * PLANE + zhi)))
    column = []
    for k in range(1, nz):
        i = around(z + k, nz)
        hi = (i >= ZLO).astype(jnp.int32) + (i >= 2 * ZLO).astype(jnp.int32)
        column.append((short(k, nz), i, ((i - ZLO * hi) * ROW + row, y * PLANE + hi)))
    stages = ((far_first(plane), y * ROW + row), (far_first(column), z))

    def ring(dy, dz):
        j, i = around(y + dy % ny, ny), around(z + dz % nz, nz)
        hi = (i >= ZLO).astype(jnp.int32) + (i >= 2 * ZLO).astype(jnp.int32)
        return (i - ZLO * hi) * ROW + row, j * PLANE + hi

    beside = [(zlo * ROW + around(row + k, ROW), w) for k in range(1, ROW)]
    next_ones = [ring(1, 0), ring(-1, 0), ring(0, 1), ring(0, -1)]
    beside = beside + next_ones
    tokens = [
        next_ones,
        [ring(2, 0), ring(-2, 0), ring(0, 2), ring(0, -2)],
        [ring(1, 0), ring(-1, 0), ring(0, 2), ring(0, -2)],
    ]

    def send_token(i):
        for where in tokens[i]:
            pl.semaphore_signal(token.at[i], inc=1, device_id=where, device_id_type=MESH)

    def wait_token(i):
        pl.semaphore_wait(token.at[i], len(tokens[i]))

    barrier = pltpu.get_barrier_semaphore()
    for cond, other in ((below1, d - 1), (above1, d + 1), (below2, d - 2), (above2, d + 2)):
        @pl.when(cond)
        def _():
            pl.semaphore_signal(barrier, inc=1, device_id=(other, w), device_id_type=MESH)
    for where in beside:
        pl.semaphore_signal(barrier, inc=1, device_id=where, device_id_type=MESH)

    def zero(ref):
        ref[...] = jnp.zeros(ref.shape, ref.dtype)

    for a in range(3):
        zero(xb.at[a, pl.ds(OWN, EXT - OWN)])
    for cond, part1, part2 in ((below1, 0, 0), (above1, 1, 1)):
        @pl.when(jnp.logical_not(cond))
        def _():
            for a in range(3):
                zero(rblk.at[a, part1])
                zero(xb.at[a, pl.ds(part2 * GHOST, GHOST)])
            zero(crecv.at[part1])
            zero(crc.at[part1])
    even = lax.rem(d, 2) == 0
    odd = jnp.logical_not(even)
    for cond, passed, part1, part2 in ((below2, odd, 0, 2), (above2, even, 1, 3)):
        @pl.when(jnp.logical_not(cond))
        def _():
            for a in range(3):
                zero(rc2.at[a, part1])

        @pl.when(jnp.logical_not(jnp.logical_and(cond, passed)))
        def _():
            for a in range(3):
                zero(xb.at[a, pl.ds(part2 * GHOST, GHOST)])
    zero(pst)
    zero(cst)

    loads[4].wait()
    for c in range(CELLS):
        nodes = nodes_ref[pl.ds(c, 1), :]
        nodes = jnp.where(nodes < GHOST, nodes, jnp.where(nodes >= GHOST + OWN, nodes - OWN, nodes + GHOST))
        rows = lax.broadcasted_iota(jnp.int32, (EXT, NPC), 0)
        scat[:, c * NPC:(c + 1) * NPC] = jnp.where(rows == nodes, 1.0, 0.0).astype(BF16)

    loads[5].wait()
    loads[6].wait()
    loads[0].wait()
    for k in range(3):
        for j in range(ATOM_HOME):
            i = (k * ATOM_HOME + j) * SLOT
            pst[pl.ds(i, NPROJ), pl.ds(0, SUP)] = pin[0, k, :, j, :].astype(F32)
            live = jnp.where(j < counts_ref[0, k], 1.0, 0.0).astype(F32)
            placed = pltpu.roll(pst[pl.ds(i, SLOT), :], starts_ref[k, 0, j], axis=1)
            pst[pl.ds(i, SLOT), :] = placed * live
    pall[...] = pst[...].astype(BF16)
    col = lax.broadcasted_iota(jnp.int32, (1, 3 * ATOM_HOME * SLOT), 1)
    slot, p = lax.div(col, SLOT), lax.rem(col, SLOT)
    target = lax.div(slot, ATOM_HOME) * HOME + lax.rem(slot, ATOM_HOME) * NPROJ + p
    target = jnp.where(p < NPROJ, target, -1)
    pick = jnp.where(
        lax.broadcasted_iota(jnp.int32, (PROWS, 3 * ATOM_HOME * SLOT), 0) == target, 1.0, 0.0
    ).astype(BF16)
    gmat[pl.ds(GHOST, PROWS), :] = dot(pick, pall[...]).astype(BF16)

    loads[1].wait()
    for j in range(ATOM_HOME):
        cst[pl.ds(j * SLOT, NPROJ), pl.ds(0, NPROJ)] = cin[:, j, :]
        rows = cst[pl.ds(j * SLOT, SLOT), :]
        csn[pl.ds(j * SLOT, SLOT), :] = rows if j == 0 else pltpu.roll(rows, j * NPROJ, axis=1)

    def both(*conds):
        return functools.reduce(jnp.logical_and, conds)

    def remote(src, dst, sems, other):
        return pltpu.make_async_remote_copy(
            src_ref=src, dst_ref=dst, send_sem=sems[0], recv_sem=sems[1],
            device_id=(other, w), device_id_type=MESH,
        )

    def app_copies(a):
        def sems(i, j=None):
            return send_sem.at[a, i if j is None else j], recv_sem.at[a, i]

        low, high = vb.at[a, pl.ds(0, GHOST)], vb.at[a, pl.ds(OWN - GHOST, GHOST)]

        def x(i):
            return xb.at[a, pl.ds(i * GHOST, GHOST)]

        def g(start, rows):
            return gb.at[a, pl.ds(start, rows)]

        near = [
            (above1, below1, high, x(0), sems(0), d + 1),
            (below1, above1, low, x(1), sems(1), d - 1),
        ]
        relay = [
            (both(even, below1), both(odd, below2), x(0), x(2), sems(2, 10), d + 1),
            (both(odd, above1), both(even, above2), x(1), x(3), sems(3, 11), d - 1),
        ]
        coefs = [
            (above1, below1, g(GHOST + HOME, 2 * HOME), rblk.at[a, 0, pl.ds(0, 2 * HOME)], sems(4), d + 1),
            (below1, above1, g(GHOST, 2 * HOME), rblk.at[a, 1, pl.ds(GHOST, 2 * HOME)], sems(5), d - 1),
            (above2, below2, g(GHOST + 2 * HOME, HOME), rc2.at[a, 0], sems(6), d + 2),
            (below2, above2, g(GHOST, HOME), rc2.at[a, 1], sems(7), d - 2),
        ]
        rim_sums = [
            (above1, below1, g(LO, GHOST), rblk.at[a, 0, pl.ds(2 * HOME, GHOST)], sems(8), d + 1),
            (below1, above1, g(0, GHOST), rblk.at[a, 1, pl.ds(0, GHOST)], sems(9), d - 1),
        ]
        return near, relay, coefs, rim_sums

    def setup_copies():
        def sems(i):
            return ssend_sem.at[i], srecv_sem.at[i]

        corners = [
            (above1, below1, csend.at[1], crecv.at[0], sems(0), d + 1),
            (below1, above1, csend.at[0], crecv.at[1], sems(1), d - 1),
        ]
        couplings = [
            (above1, below1, csn, crc.at[0], sems(2), d + 1),
            (below1, above1, csn, crc.at[1], sems(3), d - 1),
        ]
        return corners, couplings

    def start(copies):
        for cond, _, src, dst, sems, other in copies:
            @pl.when(cond)
            def _():
                remote(src, dst, sems, other).start()

    def wait_recv(copies):
        for _, cond, src, dst, sems, other in copies:
            @pl.when(cond)
            def _():
                remote(src, dst, sems, other).wait_recv()

    def wait_send(copies):
        for cond, _, src, dst, sems, other in copies:
            @pl.when(cond)
            def _():
                remote(src, dst, sems, other).wait_send()

    def project(a):
        coefs = dot(gmat[GHOST:LO, :], vb[a])
        gb[a, GHOST:LO, :] = coefs.astype(BF16)
        c32[...] = coefs

    def sum_rims(a, near):
        low, high = dot(gmat[0:GHOST, :], vb[a]), dot(gmat[LO:, :], vb[a])

        @pl.when(odd)
        def _():
            wait_recv(near[0:1])
            gb[a, 0:GHOST, :] = low.astype(BF16)
            gb[a, LO:, :] = (high + dot(csend[1, 0:GHOST, 0:GHOST], xb[a, 0:GHOST, :])).astype(BF16)

        @pl.when(even)
        def _():
            wait_recv(near[1:2])
            gb[a, 0:GHOST, :] = (low + dot(csend[0, 0:GHOST, GHOST:], xb[a, GHOST:2 * GHOST, :])).astype(BF16)
            gb[a, LO:, :] = high.astype(BF16)

    def wait_linked(near):
        @pl.when(odd)
        def _():
            wait_recv(near[1:2])

        @pl.when(even)
        def _():
            wait_recv(near[0:1])

    loads[3].wait()
    vb[0] = fv[0].astype(BF16)
    project(0)
    pl.semaphore_wait(
        barrier,
        len(beside) + below1.astype(jnp.int32) + below2.astype(jnp.int32)
        + above1.astype(jnp.int32) + above2.astype(jnp.int32),
    )
    for i in (0, 2):
        start(app_copies(0)[i])
    start(setup_copies()[1])
    send_token(0)

    loads[2].wait()

    rims = 2 * GHOST
    eye = lax.broadcasted_iota(jnp.int32, (GHOST, GHOST), 0) == lax.broadcasted_iota(jnp.int32, (GHOST, GHOST), 1)

    def place(rows):
        for c in range(CELLS):
            cell = pl.ds(c * NPC, NPC)
            tcat[rows, cell] = dot(scat[rows, cell], cm[c]).astype(BF16)

    place(pl.ds(0, rims))
    rim = dot_nt(tcat[0:rims, :], scat[...])
    gmat[pl.ds(0, GHOST), :] = rim[0:GHOST, rims:].astype(BF16)
    gmat[pl.ds(LO, GHOST), :] = rim[GHOST:, rims:].astype(BF16)
    for side in range(2):
        ends = rim[side * GHOST:(side + 1) * GHOST, 0:rims]
        rounded = ends.astype(BF16)
        csend[side, 0:GHOST, :] = rounded
        left = (ends - rounded.astype(F32))[:, side * GHOST:(side + 1) * GHOST]
        left = jnp.sum(jnp.where(eye, left, 0.0), axis=0, keepdims=True)
        csend[side, GHOST:, 0:GHOST] = jnp.broadcast_to(left, (16, GHOST)).astype(BF16)

    near, relay, coefs, rim_sums = app_copies(0)
    corners, couplings = setup_copies()
    sum_rims(0, near)
    start(rim_sums)
    start(corners)
    wait_linked(near)
    start(relay)

    fmat[:, 0:rims] = rim[:, rims:].T.astype(BF16)
    place(pl.ds(rims, OWN))
    first, second = pl.ds(rims, 256), pl.ds(rims + 256, 256)
    cross = dot_nt(tcat[first, :], scat[second, :])
    amat[0:256, 256:] = cross.astype(BF16)
    amat[256:, 0:256] = cross.T.astype(BF16)

    def diagonal(block, q):
        rounded = block.astype(BF16)
        rows = pl.ds(q * GHOST, GHOST)
        amat[rows, rows] = rounded
        left = jnp.sum(jnp.where(eye, block - rounded.astype(F32), 0.0), axis=1, keepdims=True)
        dtab[rows, :] = jnp.broadcast_to(left, (GHOST, COLS))

    for half, rows in ((0, first), (1, second)):
        block = dot_nt(tcat[rows, :], scat[rows, :])
        at = half * 256
        amat[at:at + GHOST, at + GHOST:at + 256] = block[0:GHOST, GHOST:].astype(BF16)
        amat[at + GHOST:at + 256, at:at + GHOST] = block[GHOST:, 0:GHOST].astype(BF16)
        if half == 0:
            corner[0] = block[0:GHOST, 0:GHOST]
            diagonal(block[GHOST:, GHOST:], 1)
        else:
            diagonal(block[0:GHOST, 0:GHOST], 2)
            corner[1] = block[GHOST:, GHOST:]

    wait_recv(couplings)
    wait_recv(corners)
    wait_token(0)
    send_token(1)
    for side in range(2):
        at = (1 - side) * GHOST
        left = crecv[side, GHOST:, 0:GHOST].astype(F32)[0:1]
        block = corner[side] + crecv[side, 0:GHOST, at:at + GHOST].astype(F32) + jnp.where(eye, left, 0.0)
        diagonal(block, 3 * side)
    empty = jnp.zeros((ATOM_HOME * SLOT, 128), F32)
    for k, block in ((0, crc[0]), (1, csn[...]), (2, crc[1])):
        wide = jnp.concatenate([block, empty], axis=1)
        call[pl.ds(k * ATOM_HOME * SLOT, ATOM_HOME * SLOT), :] = wide if k == 0 else pltpu.roll(wide, k * HOME, axis=1)
    couple = call[...]
    couple_hi = couple.astype(BF16)
    couple_lo = (couple - couple_hi.astype(F32)).astype(BF16)
    fmat[:, rims:] = (dot_tn(pall[...], couple_hi) + dot_tn(pall[...], couple_lo)).astype(BF16)

    half_width = (upper_edge - cut_edge) / 2.0
    centre = (upper_edge + cut_edge) / 2.0
    sigma_one = half_width / (lower_edge - centre)
    gamma_ratio = 2.0 / sigma_one
    sigma_two = 1.0 / (gamma_ratio - sigma_one)
    sigma_three = 1.0 / (gamma_ratio - sigma_two)
    scales = (sigma_one / half_width, 2.0 * sigma_two / half_width, 2.0 * sigma_three / half_width)
    backs = (0.0, sigma_one * sigma_two, sigma_two * sigma_three)

    for a in range(3):
        near, relay, coefs, rim_sums = app_copies(a)
        if a > 0:
            start(near)
            project(a)
            start(coefs)
            sum_rims(a, near)
            start(rim_sums)
            wait_token(a)
            if a == 1:
                send_token(2)
        acc[...] = dot(amat[...], vb[a]) + (dtab[...] * vb[a].astype(F32) - centre * fv[a])
        if a > 0:
            wait_linked(near)
            start(relay)
        acc[...] += dot(fmat[:, 0:rims], xb[a, 0:rims, :])
        wait_recv(coefs)
        below, above = rblk[a, 0, 0:2 * HOME, :].astype(F32), rblk[a, 1, GHOST:, :].astype(F32)
        own = c32[...]
        xb[a, OWN:OWN + HOME, :] = (own[0:HOME] + below[0:HOME] + rc2[a, 0].astype(F32)).astype(BF16)
        xb[a, OWN + HOME:OWN + 2 * HOME, :] = (
            own[HOME:2 * HOME] + below[HOME:2 * HOME] + above[0:HOME]
        ).astype(BF16)
        xb[a, OWN + 2 * HOME:OWN + 3 * HOME, :] = (
            own[2 * HOME:] + above[HOME:] + rc2[a, 1].astype(F32)
        ).astype(BF16)
        acc[...] += dot(fmat[:, rims:], xb[a, OWN:, :])
        wait_recv(relay)
        wait_recv(rim_sums)
        acc[0:GHOST, :] += rblk[a, 0, 2 * HOME:, :].astype(F32) + dot(
            crecv[0, 0:GHOST, 0:GHOST], xb[a, 2 * GHOST:3 * GHOST, :]
        )
        acc[OWN - GHOST:, :] += rblk[a, 1, 0:GHOST, :].astype(F32) + dot(
            crecv[1, 0:GHOST, GHOST:], xb[a, 3 * GHOST:4 * GHOST, :]
        )
        new = acc[...] * scales[a]
        if a > 0:
            new = new - backs[a] * fv[a - 1]
        if a == 2:
            out_ref[...] = new
        else:
            fv[a + 1] = new
            vb[a + 1] = new.astype(BF16)

    mine = jnp.sum(new * new, axis=0, keepdims=True)
    base, sent = 0, []
    for (peers, me), sums in zip(stages, (part, zsum)):
        sums[me] = mine
        for k, (_, where) in enumerate(peers):
            copy = pltpu.make_async_remote_copy(
                src_ref=sums.at[me], dst_ref=sums.at[me],
                send_sem=nsend.at[base + k], recv_sem=nrecv.at[base + me],
                device_id=where, device_id_type=MESH,
            )
            copy.start()
            sent.append(copy)
        if base == 0:
            for a in range(3):
                for group in app_copies(a):
                    wait_send(group)
            for group in setup_copies():
                wait_send(group)
        else:
            for copy in sent:
                copy.wait_send()
        for k, (i, where) in reversed(list(enumerate(peers))):
            pltpu.make_async_remote_copy(
                src_ref=sums.at[i], dst_ref=sums.at[i],
                send_sem=nsend.at[base + k], recv_sem=nrecv.at[base + i],
                device_id=where, device_id_type=MESH,
            ).wait_recv()
        size = len(peers) + 1
        terms = [sums[i] for i in range(size)]
        while len(terms) > 1:
            terms = [sum(terms[i:i + 2][1:], terms[i]) for i in range(0, len(terms), 2)]
        mine = terms[0]
        base += size
    norm_ref[...] = jnp.sqrt(jnp.sum(mine, axis=1, keepdims=True))


def solution(mesh):
    ny = mesh.shape["wf"] // PLANE
    members = ROW * ny + ZLO * PLANE

    def local(wavefunctions, cell_matrix, cell_nodes, home_counts, atom_start, projectors, coupling):
        hbm = pl.BlockSpec(memory_space=pl.ANY)
        vmem = pl.BlockSpec(memory_space=pltpu.VMEM)
        filtered, norm = pl.pallas_call(
            functools.partial(kernel, ny),
            out_shape=(
                pltpu.VMEM((OWN, COLS), F32),
                pltpu.VMEM((1, 1), F32),
            ),
            in_specs=[hbm] * 7,
            out_specs=(vmem, vmem),
            scratch_shapes=[
                pltpu.VMEM((4, OWN, COLS), F32),
                pltpu.VMEM((3, OWN, COLS), BF16),
                pltpu.VMEM((3, GROWS, COLS), BF16),
                pltpu.VMEM((3, EXT, COLS), BF16),
                pltpu.VMEM((3, 2, BLK, COLS), BF16),
                pltpu.VMEM((3, 2, HOME, COLS), BF16),
                pltpu.VMEM((PROWS, COLS), F32),
                pltpu.VMEM((OWN, COLS), F32),
                pltpu.VMEM((CELLS, NPC, NPC), BF16),
                pltpu.VMEM((EXT, CELLS * NPC), BF16),
                pltpu.VMEM((EXT, CELLS * NPC), BF16),
                pltpu.VMEM((GROWS, OWN), BF16),
                pltpu.VMEM((OWN, OWN), BF16),
                pltpu.VMEM((OWN, COLS), F32),
                pltpu.VMEM((OWN, 2 * GHOST + 256), BF16),
                pltpu.VMEM((2, GHOST, GHOST), F32),
                pltpu.VMEM((2, GHOST + 16, 2 * GHOST), BF16),
                pltpu.VMEM((2, GHOST + 16, 2 * GHOST), BF16),
                pltpu.VMEM((CELLS, NPC), jnp.int32),
                pltpu.SMEM((1, 3), jnp.int32),
                pltpu.SMEM((3, 1, ATOM_HOME), jnp.int32),
                pltpu.VMEM((1, 3, NPROJ, ATOM_HOME, SUP), BF16),
                pltpu.VMEM((3 * ATOM_HOME * SLOT, OWN), F32),
                pltpu.VMEM((3 * ATOM_HOME * SLOT, OWN), BF16),
                pltpu.VMEM((NPROJ, ATOM_HOME, NPROJ), F32),
                pltpu.VMEM((ATOM_HOME * SLOT, 128), F32),
                pltpu.VMEM((ATOM_HOME * SLOT, 128), F32),
                pltpu.VMEM((2, ATOM_HOME * SLOT, 128), F32),
                pltpu.VMEM((3 * ATOM_HOME * SLOT, 256), F32),
                pltpu.VMEM((ROW * ny, 1, COLS), F32),
                pltpu.VMEM((ZLO * PLANE, 1, COLS), F32),
                pltpu.SemaphoreType.DMA((7,)),
                pltpu.SemaphoreType.DMA((3, 12)),
                pltpu.SemaphoreType.DMA((3, 10)),
                pltpu.SemaphoreType.DMA((4,)),
                pltpu.SemaphoreType.DMA((4,)),
                pltpu.SemaphoreType.DMA((members,)),
                pltpu.SemaphoreType.DMA((members,)),
                pltpu.SemaphoreType.REGULAR((3,)),
            ],
            compiler_params=pltpu.CompilerParams(collective_id=0, has_side_effects=True),
            name="chebyshev",
        )(
            wavefunctions, cell_matrix, cell_nodes, home_counts, atom_start.transpose(1, 0, 2),
            projectors.transpose(0, 1, 3, 2, 4), coupling.transpose(1, 0, 2),
        )
        return filtered, norm.reshape(())

    return jax.shard_map(
        local,
        mesh=mesh,
        in_specs=(
            P("dom", "wf"),
            P("dom", None, None),
            P("dom", None),
            P("dom", None),
            P("dom", None, None),
            P("dom", None, None, None, None),
            P("dom", None, None),
        ),
        out_specs=(P("dom", "wf"), P()),
        check_vma=False,
    )
```
